256 devices in a mesh: row: 32 (over z, x), col: 8 (over y, core).
Axes of the slice: x: 4, y: 4, z: 8, core: 2. Of those that a mesh axis runs over, the one named last changes fastest.
Arguments:
- rhs: float32 [384, 512, 512], P('col', 'row'), may hold values from -6 to 6
- lower: float32 [384], replicated, may hold values from 0.5 to 2
- upper: float32 [384], replicated, may hold values from 0.5 to 2
Outputs:
- pressure: float32 [384, 512, 512], P('col', 'row')
The draws below stay inside these ranges and needn't reach their ends.
All inputs are finite; a program needn't handle non-finite values.
Results may differ from the reference program's by a relative error of at most 0.0003.
Values sent between devices are 32-bit elements; how exact they have to be, the bound alone decides.
No kernel may reach another device: no remote copies, remote signals or barrier semaphores. Data moves between devices by JAX's collectives and lax.ppermute only.
A program may use at most 64 MiB of HBM per device.

```python
import math
import jax
import jax.numpy as jnp
from jax import lax

NX = 512
NY = 384
NZ = 512


def levels(stream_key, extent, cuts, smallest, largest):
    def one(position, parts):
        heights = jax.random.uniform(jax.random.fold_in(jax.random.fold_in(stream_key, 6), position), (parts,), jnp.float32, smallest / len(cuts), largest / len(cuts))
        return jnp.repeat(jnp.exp(heights), extent[position] // parts).reshape((-1,) + (1,) * (len(extent) - position - 1))

    level = one(*cuts[0])
    for cut in cuts[1:]:
        level = level * one(*cut)
    return level


def normal_values(stream_key, shape, scale, reach, shards=(), dtype=jnp.bfloat16):
    drawn = jax.random.normal(stream_key, shape, jnp.float32) * scale
    if len(shards) > 0:
        drawn = levels(stream_key, shape, shards, -0.22, 0.18) * drawn
    return jnp.clip(drawn, min=-reach, max=reach).astype(dtype)


def setup_inputs(seed: int = 0) -> dict:
    key_of = jax.random.split(jax.random.key(seed), 4)
    return {
        "rhs": normal_values(key_of[0], (NY, NZ, NX), 1.0, 6.0, ((0, 8), (1, 32)), jnp.float32),
        "lower": jnp.clip(jnp.exp(jax.random.uniform(key_of[1], (NY,), jnp.float32, math.log(0.5), math.log(2.0))), 0.5, 2.0),
        "upper": jnp.clip(jnp.exp(jax.random.uniform(key_of[2], (NY,), jnp.float32, math.log(0.5), math.log(2.0))), 0.5, 2.0),
    }


stream_weight = 0.04
span_weight = 0.16
shift_value = 2.0e-4


def wave_square(stream_index, span_index):
    stream_angle = (2.0 * math.pi / NX) * stream_index.astype(jnp.float32)
    span_angle = (2.0 * math.pi / NZ) * span_index.astype(jnp.float32)
    stream_part = stream_weight * (2.0 - 2.0 * jnp.cos(stream_angle))
    span_part = span_weight * (2.0 - 2.0 * jnp.cos(span_angle))
    return stream_part[None, :] + span_part[:, None]


def reference(rhs, lower, upper):
    half = NX // 2

    def forward_plane(plane):
        along = jnp.fft.rfft(plane, axis=1)[:, :half]
        both = jnp.fft.fft(along, axis=0) / (NX * NZ)
        return jnp.real(both), jnp.imag(both)

    spec_real, spec_imag = lax.map(forward_plane, rhs)
    waves = wave_square(jnp.arange(half), jnp.arange(NZ))

    def descend(carry, inputs):
        ratio, real_part, imag_part = carry
        low, high, source_real, source_imag = inputs
        pivot = -(low + high) - waves - shift_value - low * ratio
        ratio = high / pivot
        real_part = (source_real - low * real_part) / pivot
        imag_part = (source_imag - low * imag_part) / pivot
        return (ratio, real_part, imag_part), (ratio, real_part, imag_part)

    zero_plane = jnp.zeros((NZ, half), jnp.float32)
    unused, (ratios, fwd_real, fwd_imag) = lax.scan(descend, (zero_plane, zero_plane, zero_plane), (lower, upper, spec_real, spec_imag))

    def ascend(carry, inputs):
        real_next, imag_next = carry
        ratio, real_part, imag_part = inputs
        real_part = real_part - ratio * real_next
        imag_part = imag_part - ratio * imag_next
        return (real_part, imag_part), (real_part, imag_part)

    unused_two, (sol_real, sol_imag) = lax.scan(ascend, (zero_plane, zero_plane), (ratios, fwd_real, fwd_imag), reverse=True)

    def inverse_plane(planes):
        real_plane, imag_plane = planes
        spectrum = lax.complex(real_plane, imag_plane)
        along = jnp.fft.ifft(spectrum, axis=0) * NZ
        padded = jnp.concatenate([along, jnp.zeros_like(along[:, :1])], axis=1)
        return jnp.fft.irfft(padded, n=NX, axis=1) * NX

    return lax.map(inverse_plane, (sol_real, sol_imag))
```

```python
import math

import jax
import jax.numpy as jnp
import ml_dtypes
import numpy as np
from jax import lax
from jax.experimental import pallas as pl
from jax.experimental.pallas import tpu as pltpu
from jax.sharding import PartitionSpec as P

stream_weight = 0.04
span_weight = 0.16
shift_value = 0.0002


def split_table(values):
    high = values.astype(ml_dtypes.bfloat16)
    low = (values - high.astype(np.float64)).astype(ml_dtypes.bfloat16)
    return jnp.asarray(high), jnp.asarray(low)


def stream_table(nx_len, groups):
    modes = nx_len // 2 // groups
    points = np.arange(nx_len)
    wave = np.arange(groups * modes).reshape(groups, 1, modes, 1)
    angle = 2.0 * math.pi / nx_len * (wave * points % nx_len)
    table = np.concatenate([np.cos(angle), -np.sin(angle)], axis=1)
    return split_table(table.reshape(nx_len, nx_len))


def span_table(nz_len):
    half = nz_len // 2
    points = np.arange(nz_len)[:, None]
    wave = np.arange(half)[None, :]
    angle = 2.0 * math.pi / nz_len * (points * wave % nz_len)
    sines = np.sin(angle)
    sines[:, 0] = np.where(np.arange(nz_len) % 2 == 0, 1.0, -1.0)
    return split_table(np.concatenate([np.cos(angle), sines], axis=1))


def wave_square(stream_index, span_index, nx_len, nz_len):
    stream_angle = 2.0 * math.pi / nx_len * stream_index.astype(jnp.float32)
    span_angle = 2.0 * math.pi / nz_len * span_index.astype(jnp.float32)
    stream_part = stream_weight * (2.0 - 2.0 * jnp.cos(stream_angle))
    span_part = span_weight * (2.0 - 2.0 * jnp.cos(span_angle))
    return stream_part[:, None] + span_part[None, :]


def halves(values):
    high = values.astype(jnp.bfloat16)
    low = (values - high.astype(jnp.float32)).astype(jnp.bfloat16)
    return high, low


def dot3(a_high, a_low, b_high, b_low, dims):
    def one(a, b):
        return lax.dot_general(a, b, (dims, ((), ())), preferred_element_type=jnp.float32)

    return one(a_high, b_high) + (one(a_high, b_low) + one(a_low, b_high))


def swap_groups(tiles, width):
    count = len(tiles)
    lanes = count * width
    tiles = list(tiles)
    group = lax.broadcasted_iota(jnp.int32, tiles[0].shape, 1) // width
    bit = count // 2
    while bit:
        upper = (group & bit) != 0
        for first in range(count):
            if first & bit:
                continue
            a, b = tiles[first], tiles[first | bit]
            tiles[first] = jnp.where(upper, pltpu.roll(b, width * bit, 1), a)
            tiles[first | bit] = jnp.where(upper, b, pltpu.roll(a, lanes - width * bit, 1))
        bit //= 2
    return tiles


def both(values):
    return jnp.concatenate([values, values], axis=0)


def stream_forward(rhs_ref, high_ref, low_ref, out_ref):
    rows, span, nx_len = rhs_ref.shape
    high, low = halves(rhs_ref[...].reshape(rows * span, nx_len))
    out = dot3(high_ref[...], low_ref[...], high, low, ((1,), (1,)))
    out_ref[...] = out.reshape(out_ref.shape)


def stream_inverse(piece_ref, high_ref, low_ref, out_ref):
    groups, parts, cells = piece_ref.shape
    flat = piece_ref[...].reshape(groups * parts, cells)
    high, low = halves(flat.T)
    out = dot3(high, low, high_ref[...], low_ref[...], ((1,), (0,)))
    out_ref[...] = out.reshape(out_ref.shape)


def factor(place_ref, lower_ref, upper_ref, waves_ref, down_ref, up_ref, carry_down_ref, carry_up_ref, close_ref, start_ref):
    rows = down_ref.shape[0]
    blocks = carry_down_ref.shape[0]
    total = rows * blocks
    sigma = waves_ref[...]
    one = jnp.ones_like(sigma)
    step = 8

    def step_down(row, numer, denom):
        numer = lower_ref[row] * numer + sigma * denom
        return numer, numer + upper_ref[row] * denom

    def step_up(row, numer, denom):
        numer = upper_ref[row] * numer + sigma * denom
        return numer, numer + lower_ref[row] * denom

    def block(index, carry):
        t_down, t_up = carry
        other = blocks - 1 - index
        start_ref[0, index] = t_down
        start_ref[1, other] = t_up

        def some(chunk, inner):
            nd, dd, nu, du, prod_l, prod_u = inner
            for k in range(step):
                row = index * rows + chunk * step + k
                back = total - 1 - row
                nd, dd = step_down(row, nd, dd)
                nu, du = step_up(back, nu, du)
                prod_l = prod_l * lower_ref[row]
                prod_u = prod_u * upper_ref[back]
            return nd, dd, nu, du, prod_l, prod_u

        unit = jnp.float32(1.0)
        nd, dd, nu, du, prod_l, prod_u = lax.fori_loop(
            0, rows // step, some, (t_down, one, t_up, one, unit, unit)
        )
        inv_d = 1.0 / dd
        inv_u = 1.0 / du
        carry_down_ref[index] = prod_l * inv_d
        carry_up_ref[other] = prod_u * inv_u
        return nd * inv_d, nu * inv_u

    lax.fori_loop(0, blocks, block, (one, one))
    place = place_ref[1]
    first = place * rows

    def own(chunk, inner):
        nd, dd, nu, du = inner
        for k in range(step):
            row = chunk * step + k
            back = rows - 1 - row
            nd, new_d = step_down(first + row, nd, dd)
            down_ref[row] = dd / new_d
            nu, new_u = step_up(first + back, nu, du)
            up_ref[back] = du / new_u
            dd, du = new_d, new_u
        return nd, dd, nu, du

    nd, dd, nu, du = lax.fori_loop(
        0, rows // step, own, (start_ref[0, place], one, start_ref[1, place], one)
    )
    t_end = nd / dd
    t_next = start_ref[1, place]
    is_last = place == blocks - 1
    inner = jnp.where(is_last, 0.0, 1.0 / (t_next + t_end * (1.0 - t_next)))
    close_ref[0] = inner
    close_ref[1] = inner * (1.0 - t_next)


def span_forward(place_ref, lower_ref, upper_ref, piece_ref, high_ref, low_ref, down_ref, up_ref, rows_ref, send_ref, left_high, left_low, keep_ref):
    groups, parts, cells = piece_ref.shape
    some, _, nz_len = rows_ref.shape
    rows = keep_ref.shape[0]
    width = nz_len // groups
    count = 128 // width
    for octet in range(some // count):
        for tile in range(groups // count):
            tiles = [piece_ref[tile * count + s, :, octet * 128 : octet * 128 + 128] for s in range(count)]
            tiles = swap_groups(tiles, width)
            for j in range(count):
                high, low = halves(tiles[j])
                row = (octet * count + j) * parts
                left_high[row : row + parts, tile * 128 : tile * 128 + 128] = high
                left_low[row : row + parts, tile * 128 : tile * 128 + 128] = low
    spec = dot3(left_high[...], left_low[...], high_ref[...], low_ref[...], ((1,), (0,)))
    spec = spec.reshape(some, parts, nz_len)
    part = lax.broadcasted_iota(jnp.int32, (parts, nz_len), 0)
    wave = lax.broadcasted_iota(jnp.int32, (parts, nz_len), 1)
    single_x = (part % (parts // 2) == 0) & (place_ref[0] == 0)
    single_z = wave % (nz_len // 2) == 0
    base = 1.0 / (nz_len * nz_len)
    scale = jnp.where(single_x, base, 2.0 * base) * jnp.where(single_z, 1.0, 2.0)
    spec = spec * scale[None]
    rows_ref[...] = spec
    index = pl.program_id(0)
    keep_ref[pl.ds(index * some, some)] = spec

    @pl.when(index == pl.num_programs(0) - 1)
    def _():
        first = place_ref[1] * rows
        step = 8

        def sweep(chunk, carry):
            down, up = carry
            for k in range(step):
                row = chunk * step + k
                back = rows - 1 - row
                down = (lower_ref[first + row] * down - keep_ref[row]) * both(down_ref[row])
                up = (upper_ref[first + back] * up - keep_ref[back]) * both(up_ref[back])
            return down, up

        zero = jnp.zeros((parts, nz_len), jnp.float32)
        down, up = lax.fori_loop(0, rows // step, sweep, (zero, zero))
        for target in range(send_ref.shape[0]):
            send_ref[target] = jnp.where(target > place_ref[1], down, up)


def span_inverse(place_ref, lower_ref, upper_ref, rows_ref, down_ref, ends_ref, carry_down_ref, carry_up_ref, close_ref, high_ref, low_ref, out_ref, grow_ref, left_high, left_low):
    groups, parts, cells = out_ref.shape
    rows, _, nz_len = rows_ref.shape
    blocks = ends_ref.shape[0]
    width = nz_len // groups
    count = 128 // width
    index = pl.program_id(0)

    @pl.when(index == 0)
    def _():
        place = place_ref[1]
        first = place * rows
        step = 8
        zero = jnp.zeros((parts, nz_len), jnp.float32)
        before = lax.fori_loop(
            0, place, lambda k, value: ends_ref[k] + both(carry_down_ref[k]) * value, zero
        )

        def climb(k, value):
            other = blocks - 1 - k
            return ends_ref[other] + both(carry_up_ref[other]) * value

        after = lax.fori_loop(0, blocks - 1 - place, climb, zero)

        def descend(chunk, value):
            for k in range(step):
                row = chunk * step + k
                value = (lower_ref[first + row] * value - rows_ref[row]) * both(down_ref[row])
                grow_ref[row] = value
            return value

        last = lax.fori_loop(0, rows // step, descend, before)
        beyond = both(close_ref[0]) * after + both(close_ref[1]) * last

        def ascend(chunk, value):
            for k in range(step):
                row = rows - 1 - (chunk * step + k)
                ratio = upper_ref[first + row] * down_ref[row]
                value = grow_ref[row] + both(ratio) * value
                high, low = halves(value)
                place_row = pl.multiple_of(row * parts, parts)
                left_high[pl.ds(place_row, parts)] = high
                left_low[pl.ds(place_row, parts)] = low
            return value

        lax.fori_loop(0, rows // step, ascend, beyond)

    some = cells // width
    start = pl.multiple_of(index * some * parts, some * parts)
    back = dot3(
        left_high[pl.ds(start, some * parts)],
        left_low[pl.ds(start, some * parts)],
        high_ref[...],
        low_ref[...],
        ((1,), (1,)),
    )
    for octet in range(some // count):
        for tile in range(groups // count):
            tiles = []
            for j in range(count):
                row = (octet * count + j) * parts
                tiles.append(back[row : row + parts, tile * 128 : tile * 128 + 128])
            tiles = swap_groups(tiles, width)
            for s in range(count):
                out_ref[tile * count + s, :, octet * 128 : octet * 128 + 128] = tiles[s]


smem = pl.BlockSpec(memory_space=pltpu.SMEM)


def whole(shape):
    return pl.BlockSpec(shape, lambda *_: (0,) * len(shape))


def local(rhs, lower, upper):
    rows, span, nx_len = rhs.shape
    groups = lax.axis_size("row")
    blocks = lax.axis_size("col")
    nz_len = span * groups
    modes = nx_len // 2 // groups
    parts = 2 * modes
    steps = 3
    some = rows // steps
    cells = some * span
    place = jnp.stack([lax.axis_index("row"), lax.axis_index("col")]).astype(jnp.int32)
    stream_high, stream_low = stream_table(nx_len, groups)
    span_high, span_low = span_table(nz_len)
    table_x = whole((nx_len, nx_len))
    table_z = whole((nz_len, nz_len))
    f32 = jnp.float32
    piece_shape = jax.ShapeDtypeStruct((groups, parts, rows * span), f32)
    piece_spec = pl.BlockSpec((groups, parts, cells), lambda i: (0, 0, i))
    field_shape = jax.ShapeDtypeStruct((rows, span, nx_len), f32)
    field_spec = pl.BlockSpec((some, span, nx_len), lambda i: (i, 0, 0))
    mode_shape = jax.ShapeDtypeStruct((rows, parts, nz_len), f32)
    mode_spec = pl.BlockSpec((some, parts, nz_len), lambda i: (i, 0, 0))
    half_spec = whole((rows, modes, nz_len))
    carry_spec = whole((blocks, modes, nz_len))
    ends_shape = jax.ShapeDtypeStruct((blocks, parts, nz_len), f32)
    ends_spec = whole((blocks, parts, nz_len))

    send = pl.pallas_call(
        stream_forward,
        grid=(steps,),
        in_specs=[field_spec, table_x, table_x],
        out_specs=piece_spec,
        out_shape=piece_shape,
        name="stream_forward",
    )(rhs, stream_high, stream_low)
    piece = lax.all_to_all(send, "row", split_axis=0, concat_axis=0, tiled=True)

    stream_index = place[0] * modes + jnp.arange(modes)
    wave = jnp.arange(nz_len) % (nz_len // 2)
    span_index = jnp.where(jnp.arange(nz_len) == nz_len // 2, nz_len // 2, wave)
    sigma = wave_square(stream_index, span_index, nx_len, nz_len) + shift_value
    down, up, carry_down, carry_up, close = pl.pallas_call(
        factor,
        in_specs=[smem, smem, smem, whole((modes, nz_len))],
        out_specs=[half_spec, half_spec, carry_spec, carry_spec, whole((2, modes, nz_len))],
        out_shape=[
            jax.ShapeDtypeStruct((rows, modes, nz_len), f32),
            jax.ShapeDtypeStruct((rows, modes, nz_len), f32),
            jax.ShapeDtypeStruct((blocks, modes, nz_len), f32),
            jax.ShapeDtypeStruct((blocks, modes, nz_len), f32),
            jax.ShapeDtypeStruct((2, modes, nz_len), f32),
        ],
        grid=(1,),
        scratch_shapes=[pltpu.VMEM((2, blocks, modes, nz_len), f32)],
        name="factor",
    )(place, lower, upper, sigma)

    left = pltpu.VMEM((some * parts, nz_len), jnp.bfloat16)
    modes_rows, ends = pl.pallas_call(
        span_forward,
        grid=(steps,),
        in_specs=[smem, smem, smem, piece_spec, table_z, table_z, half_spec, half_spec],
        out_specs=[mode_spec, ends_spec],
        out_shape=[mode_shape, ends_shape],
        scratch_shapes=[left, left, pltpu.VMEM((rows, parts, nz_len), f32)],
        name="span_forward",
    )(place, lower, upper, piece, span_high, span_low, down, up)
    ends = lax.all_to_all(ends, "col", split_axis=0, concat_axis=0, tiled=True)

    left = pltpu.VMEM((rows * parts, nz_len), jnp.bfloat16)
    send = pl.pallas_call(
        span_inverse,
        grid=(steps,),
        in_specs=[smem, smem, smem, whole((rows, parts, nz_len)), half_spec, ends_spec, carry_spec, carry_spec, whole((2, modes, nz_len)), table_z, table_z],
        out_specs=piece_spec,
        out_shape=piece_shape,
        scratch_shapes=[pltpu.VMEM((rows, parts, nz_len), f32), left, left],
        name="span_inverse",
    )(place, lower, upper, modes_rows, down, ends, carry_down, carry_up, close, span_high, span_low)
    piece = lax.all_to_all(send, "row", split_axis=0, concat_axis=0, tiled=True)

    return pl.pallas_call(
        stream_inverse,
        grid=(steps,),
        in_specs=[piece_spec, table_x, table_x],
        out_specs=field_spec,
        out_shape=field_shape,
        name="stream_inverse",
    )(piece, stream_high, stream_low)


def solution(mesh):
    return jax.shard_map(
        local,
        mesh=mesh,
        in_specs=(P("col", "row", None), P(), P()),
        out_specs=P("col", "row", None),
        check_vma=False,
    )
```

```python
import math

import jax
import jax.numpy as jnp
import ml_dtypes
import numpy as np
from jax import lax
from jax.experimental import pallas as pl
from jax.experimental.pallas import tpu as pltpu
from jax.sharding import PartitionSpec as P

stream_weight = 0.04
span_weight = 0.16
shift_value = 0.0002


def split_table(values):
    high = values.astype(ml_dtypes.bfloat16)
    low = (values - high.astype(np.float64)).astype(ml_dtypes.bfloat16)
    return jnp.asarray(high), jnp.asarray(low)


def stream_table(nx_len, groups):
    half = nx_len // 2
    modes = half // groups
    points = np.arange(half)
    wave = 2 * np.arange(half // 2).reshape(1, -1, 1, modes, 1) + np.arange(2).reshape(2, 1, 1, 1, 1)
    angle = 2.0 * math.pi / nx_len * (wave * points % nx_len)
    table = np.concatenate([np.cos(angle), -np.sin(angle)], axis=2)
    return split_table(table.reshape(2, half, half))


def span_waves(nz_len):
    even = np.arange(0, nz_len // 2, 2)
    top = np.where(even == 0, nz_len // 2, even)
    return np.concatenate([even, top, even + 1, even + 1])


def span_table(nz_len):
    half = nz_len // 2
    points = np.arange(half)[:, None]
    wave = span_waves(nz_len)[None, :]
    angle = 2.0 * math.pi / nz_len * (points * wave % nz_len)
    index = np.arange(nz_len)[None, :]
    cosine = (index % half < half // 2) | (index == half // 2)
    table = np.where(cosine, np.cos(angle), np.sin(angle))
    return split_table(np.stack([table[:, :half], table[:, half:]]))


def wave_square(stream_index, span_index, nx_len, nz_len):
    stream_angle = 2.0 * math.pi / nx_len * stream_index.astype(jnp.float32)
    span_angle = 2.0 * math.pi / nz_len * span_index.astype(jnp.float32)
    stream_part = stream_weight * (2.0 - 2.0 * jnp.cos(stream_angle))
    span_part = span_weight * (2.0 - 2.0 * jnp.cos(span_angle))
    return stream_part[:, None] + span_part[None, :]


def halves(values):
    high = values.astype(jnp.bfloat16)
    low = (values - high.astype(jnp.float32)).astype(jnp.bfloat16)
    return high, low


def dot3(a_high, a_low, b_high, b_low, dims):
    def one(a, b):
        return lax.dot_general(a, b, (dims, ((), ())), preferred_element_type=jnp.float32)

    return one(a_high, b_high) + (one(a_high, b_low) + one(a_low, b_high))


def swap_groups(tiles, width):
    count = len(tiles)
    lanes = count * width
    tiles = list(tiles)
    group = lax.broadcasted_iota(jnp.int32, tiles[0].shape, 1) // width
    bit = count // 2
    while bit:
        upper = (group & bit) != 0
        for first in range(count):
            if first & bit:
                continue
            a, b = tiles[first], tiles[first | bit]
            tiles[first] = jnp.where(upper, pltpu.roll(b, width * bit, 1), a)
            tiles[first | bit] = jnp.where(upper, b, pltpu.roll(a, lanes - width * bit, 1))
        bit //= 2
    return tiles


def both(values):
    return jnp.concatenate([values, values], axis=0)


def stream_forward(rhs_ref, high_ref, low_ref, out_ref):
    rows, span, nx_len = rhs_ref.shape
    groups = out_ref.shape[0]
    cells = rows * span
    half = nx_len // 2
    field = rhs_ref[...].reshape(cells, nx_len)
    first, second = field[:, :half], field[:, half:]
    for parity, folded in enumerate((first + second, first - second)):
        high, low = halves(folded)
        out = dot3(high_ref[parity], low_ref[parity], high, low, ((1,), (1,)))
        place = parity * groups // 2
        out_ref[place : place + groups // 2] = out.reshape(groups // 2, -1, cells)


def stream_inverse(piece_ref, high_ref, low_ref, out_ref):
    rows, span, nx_len = out_ref.shape
    groups = piece_ref.shape[0]
    cells = rows * span
    half = nx_len // 2
    start = pl.multiple_of(pl.program_id(0) * cells, cells)
    outs = []
    for parity in range(2):
        place = parity * groups // 2
        flat = piece_ref[place : place + groups // 2, :, pl.ds(start, cells)].reshape(half, cells)
        high, low = halves(flat.T)
        outs.append(dot3(high, low, high_ref[parity], low_ref[parity], ((1,), (0,))))
    even, odd = outs
    out_ref[:, :, :half] = (even + odd).reshape(rows, span, half)
    out_ref[:, :, half:] = (even - odd).reshape(rows, span, half)


def factor(place_ref, lower_ref, upper_ref, waves_ref, both_ref, carry_down_ref, carry_up_ref, close_ref, start_ref):
    rows = both_ref.shape[1]
    blocks = carry_down_ref.shape[0]
    total = rows * blocks
    sigma = waves_ref[...]
    one = jnp.ones_like(sigma)
    step = 8

    def step_down(row, numer, denom):
        numer = lower_ref[row] * numer + sigma * denom
        return numer, numer + upper_ref[row] * denom

    def step_up(row, numer, denom):
        numer = upper_ref[row] * numer + sigma * denom
        return numer, numer + lower_ref[row] * denom

    def block(index, carry):
        t_down, t_up = carry
        other = blocks - 1 - index
        start_ref[0, index] = t_down
        start_ref[1, other] = t_up

        def some(chunk, inner):
            nd, dd, nu, du, prod_l, prod_u = inner
            for k in range(step):
                row = index * rows + chunk * step + k
                back = total - 1 - row
                nd, dd = step_down(row, nd, dd)
                nu, du = step_up(back, nu, du)
                prod_l = prod_l * lower_ref[row]
                prod_u = prod_u * upper_ref[back]
            return nd, dd, nu, du, prod_l, prod_u

        unit = jnp.float32(1.0)
        nd, dd, nu, du, prod_l, prod_u = lax.fori_loop(
            0, rows // step, some, (t_down, one, t_up, one, unit, unit)
        )
        inv_d = 1.0 / dd
        inv_u = 1.0 / du
        carry_down_ref[index] = prod_l * inv_d
        carry_up_ref[other] = prod_u * inv_u
        return nd * inv_d, nu * inv_u

    lax.fori_loop(0, blocks, block, (one, one))
    place = place_ref[1]
    first = place * rows

    def own(chunk, inner):
        nd, dd, nu, du = inner
        for k in range(step):
            row = chunk * step + k
            back = rows - 1 - row
            nd, new_d = step_down(first + row, nd, dd)
            both_ref[0, row] = dd / new_d
            nu, new_u = step_up(first + back, nu, du)
            both_ref[1, back] = du / new_u
            dd, du = new_d, new_u
        return nd, dd, nu, du

    nd, dd, nu, du = lax.fori_loop(
        0, rows // step, own, (start_ref[0, place], one, start_ref[1, place], one)
    )
    t_end = nd / dd
    t_next = start_ref[1, place]
    is_last = place == blocks - 1
    inner = jnp.where(is_last, 0.0, 1.0 / (t_next + t_end * (1.0 - t_next)))
    close_ref[0] = inner
    close_ref[1] = inner * (1.0 - t_next)


def span_forward(place_ref, lower_ref, upper_ref, piece_ref, high_ref, low_ref, factor_ref, rows_ref, send_ref, left_ref):
    groups, parts, cells = piece_ref.shape
    rows, _, nz_len = rows_ref.shape
    half = nz_len // 2
    width = nz_len // groups
    count = 128 // width
    some = left_ref.shape[1] // parts
    part = lax.broadcasted_iota(jnp.int32, (parts, half), 0)
    wave = lax.broadcasted_iota(jnp.int32, (parts, half), 1)
    single_x = (part % (parts // 2) == 0) & (place_ref[0] == 0)
    single_z = wave % (half // 2) == 0
    base = 1.0 / (nz_len * nz_len)
    scale_odd = jnp.where(single_x, 2.0 * base, 4.0 * base)
    scale_even = scale_odd * jnp.where(single_z, 0.5, 1.0)

    def transform(index, carry):
        for octet in range(some // count):
            lane = pl.multiple_of(index * (some * width) + octet * 128, 128)
            for tile in range(groups // count // 2):
                first = [piece_ref[tile * count + s, :, pl.ds(lane, 128)] for s in range(count)]
                second = [piece_ref[groups // 2 + tile * count + s, :, pl.ds(lane, 128)] for s in range(count)]
                for parity in range(2):
                    tiles = [a - b if parity else a + b for a, b in zip(first, second)]
                    tiles = swap_groups(tiles, width)
                    for j in range(count):
                        row = (octet * count + j) * parts
                        left_ref[parity, row : row + parts, tile * 128 : tile * 128 + 128] = tiles[j]
        for parity, scale in enumerate((scale_even, scale_odd)):
            high, low = halves(left_ref[parity])
            spec = dot3(high, low, high_ref[parity], low_ref[parity], ((1,), (0,)))
            spec = spec.reshape(some, parts, half) * scale[None]
            rows_ref[pl.ds(index * some, some), :, parity * half : parity * half + half] = spec
        return carry

    lax.fori_loop(0, rows // some, transform, 0)
    first = place_ref[1] * rows
    step = 8

    def sweep(chunk, carry):
        down, up = carry
        for k in range(step):
            row = chunk * step + k
            back = rows - 1 - row
            down = (lower_ref[first + row] * down - rows_ref[row]) * both(factor_ref[0, row])
            up = (upper_ref[first + back] * up - rows_ref[back]) * both(factor_ref[1, back])
        return down, up

    zero = jnp.zeros((parts, nz_len), jnp.float32)
    down, up = lax.fori_loop(0, rows // step, sweep, (zero, zero))
    for target in range(send_ref.shape[0]):
        send_ref[target] = jnp.where(target > place_ref[1], down, up)


def span_inverse(place_ref, lower_ref, upper_ref, rows_ref, factor_ref, ends_ref, carry_down_ref, carry_up_ref, close_ref, high_ref, low_ref, out_ref, grow_ref):
    groups, parts, cells = out_ref.shape
    rows, _, nz_len = rows_ref.shape
    blocks = ends_ref.shape[0]
    half = nz_len // 2
    width = nz_len // groups
    count = 128 // width
    some = 16
    place = place_ref[1]
    first = place * rows
    step = 8
    zero = jnp.zeros((parts, nz_len), jnp.float32)
    before = lax.fori_loop(
        0, place, lambda k, value: ends_ref[k] + both(carry_down_ref[k]) * value, zero
    )

    def climb(k, value):
        other = blocks - 1 - k
        return ends_ref[other] + both(carry_up_ref[other]) * value

    after = lax.fori_loop(0, blocks - 1 - place, climb, zero)

    def descend(chunk, value):
        for k in range(step):
            row = chunk * step + k
            value = (lower_ref[first + row] * value - rows_ref[row]) * both(factor_ref[0, row])
            grow_ref[row] = value
        return value

    last = lax.fori_loop(0, rows // step, descend, before)
    beyond = both(close_ref[0]) * after + both(close_ref[1]) * last

    def ascend(chunk, value):
        for k in range(step):
            row = rows - 1 - (chunk * step + k)
            ratio = upper_ref[first + row] * factor_ref[0, row]
            value = grow_ref[row] + both(ratio) * value
            grow_ref[row] = value
        return value

    lax.fori_loop(0, rows // step, ascend, beyond)

    def transform(index, carry):
        backs = []
        for parity in range(2):
            left = grow_ref[pl.ds(index * some, some), :, parity * half : parity * half + half]
            high, low = halves(left.reshape(some * parts, half))
            backs.append(dot3(high, low, high_ref[parity], low_ref[parity], ((1,), (1,))))
        even, odd = backs
        for part, back in enumerate((even + odd, even - odd)):
            for octet in range(some // count):
                lane = pl.multiple_of(index * (some * width) + octet * 128, 128)
                for tile in range(groups // count // 2):
                    tiles = []
                    for j in range(count):
                        row = (octet * count + j) * parts
                        tiles.append(back[row : row + parts, tile * 128 : tile * 128 + 128])
                    tiles = swap_groups(tiles, width)
                    for s in range(count):
                        out_ref[part * groups // 2 + tile * count + s, :, pl.ds(lane, 128)] = tiles[s]
        return carry

    lax.fori_loop(0, rows // some, transform, 0)


smem = pl.BlockSpec(memory_space=pltpu.SMEM)


vmem = pl.BlockSpec(memory_space=pltpu.VMEM)


def local(rhs, lower, upper):
    rows, span, nx_len = rhs.shape
    groups = lax.axis_size("row")
    blocks = lax.axis_size("col")
    nz_len = span * groups
    modes = nx_len // 2 // groups
    parts = 2 * modes
    steps = 3
    some = rows // steps
    place = jnp.stack([lax.axis_index("row"), lax.axis_index("col")]).astype(jnp.int32)
    stream_high, stream_low = stream_table(nx_len, groups)
    span_high, span_low = span_table(nz_len)
    f32 = jnp.float32
    params = pltpu.CompilerParams(vmem_limit_bytes=16 * 1024 * 1024)

    def on_chip(*shape):
        return pltpu.VMEM(shape, f32)

    def on_hbm(value):
        return pltpu.with_memory_space_constraint(value, pltpu.HBM)

    table_spec = pl.BlockSpec((2, nx_len // 2, nx_len // 2), lambda i: (0, 0, 0))
    field_spec = pl.BlockSpec((some, span, nx_len), lambda i: (i, 0, 0))
    piece_shape = on_chip(groups, parts, rows * span)

    def exchange(value, axis):
        return lax.all_to_all(value, axis, split_axis=0, concat_axis=0, tiled=True)

    send = pl.pallas_call(
        stream_forward,
        grid=(steps,),
        in_specs=[field_spec, table_spec, table_spec],
        out_specs=pl.BlockSpec((groups, parts, some * span), lambda i: (0, 0, i)),
        out_shape=jax.ShapeDtypeStruct((groups, parts, rows * span), f32),
        compiler_params=params,
        name="stream_forward",
    )(on_hbm(rhs), on_hbm(stream_high), on_hbm(stream_low))
    piece = exchange(send, "row")

    order = place[0] * modes + jnp.arange(modes)
    quarter = nx_len // 4
    stream_index = 2 * (order % quarter) + order // quarter
    span_index = jnp.asarray(span_waves(nz_len).astype(np.int32))
    sigma = wave_square(stream_index, span_index, nx_len, nz_len) + shift_value
    factors, carry_down, carry_up, close = pl.pallas_call(
        factor,
        in_specs=[smem, smem, smem, vmem],
        out_specs=[vmem] * 4,
        out_shape=[
            on_chip(2, rows, modes, nz_len),
            on_chip(blocks, modes, nz_len),
            on_chip(blocks, modes, nz_len),
            on_chip(2, modes, nz_len),
        ],
        scratch_shapes=[on_chip(2, blocks, modes, nz_len)],
        compiler_params=params,
        name="factor",
    )(place, lower, upper, sigma)

    mode_rows, ends = pl.pallas_call(
        span_forward,
        in_specs=[smem, smem, smem] + [vmem] * 4,
        out_specs=[vmem, vmem],
        out_shape=[on_chip(rows, parts, nz_len), on_chip(blocks, parts, nz_len)],
        scratch_shapes=[on_chip(2, some * parts, nz_len // 2)],
        compiler_params=params,
        name="span_forward",
    )(place, lower, upper, piece, span_high, span_low, factors)
    ends = exchange(ends, "col")

    send = pl.pallas_call(
        span_inverse,
        in_specs=[smem, smem, smem] + [vmem] * 8,
        out_specs=vmem,
        out_shape=piece_shape,
        scratch_shapes=[on_chip(rows, parts, nz_len)],
        compiler_params=params,
        name="span_inverse",
    )(place, lower, upper, mode_rows, factors, ends, carry_down, carry_up, close, span_high, span_low)
    piece = exchange(send, "row")

    return pl.pallas_call(
        stream_inverse,
        grid=(steps,),
        in_specs=[vmem, vmem, vmem],
        out_specs=field_spec,
        out_shape=jax.ShapeDtypeStruct((rows, span, nx_len), f32),
        compiler_params=params,
        name="stream_inverse",
    )(piece, stream_high, stream_low)


def solution(mesh):
    return jax.shard_map(
        local,
        mesh=mesh,
        in_specs=(P("col", "row", None), P(), P()),
        out_specs=P("col", "row", None),
        check_vma=False,
    )
```

```python
import math

import jax
import jax.numpy as jnp
import ml_dtypes
import numpy as np
from jax import lax
from jax.experimental import pallas as pl
from jax.experimental.pallas import tpu as pltpu
from jax.sharding import PartitionSpec as P

stream_weight = 0.04
span_weight = 0.16
shift_value = 0.0002


def split_table(values):
    high = values.astype(ml_dtypes.bfloat16)
    low = (values - high.astype(np.float64)).astype(ml_dtypes.bfloat16)
    return jnp.asarray(np.stack([high, low]))


def stream_table(nx_len):
    half = nx_len // 2
    wave = 2 * np.arange(half // 2)[None, None, :] + np.arange(2)[:, None, None]
    angle = 2.0 * math.pi / nx_len * (np.arange(half)[None, :, None] * wave % nx_len)
    return split_table(np.concatenate([np.cos(angle), -np.sin(angle)], axis=2))


def span_waves(nz_len):
    half = nz_len // 2
    wave = np.arange(half)
    return np.concatenate([wave, np.where(wave == 0, half, wave)])


def span_basis(points, nz_len):
    angle = 2.0 * math.pi / nz_len * (points[:, None] * span_waves(nz_len)[None, :] % nz_len)
    cosine = np.arange(nz_len)[None, :] <= nz_len // 2
    return np.where(cosine, np.cos(angle), np.sin(angle))


def plane_table(nz_len, groups):
    span = nz_len // groups
    block = np.arange(groups) * span
    return split_table(span_basis(np.concatenate([block - 1, block + span]) % nz_len, nz_len))


def cell_table(nz_len, groups):
    return split_table(span_basis(np.arange(nz_len).reshape(groups, -1).T.reshape(-1), nz_len))


def sine_matrix(span):
    index = np.arange(1, span + 1)
    return np.sin(math.pi / (span + 1) * index[:, None] * index[None, :])


def edge_table(span, some, steps):
    sines = sine_matrix(span) * (2.0 / (span + 1))
    eye = np.eye(some)
    table = np.zeros((steps, 2 * some + span, some * span))
    for chunk in range(steps):
        table[chunk, :some] = np.kron(eye, sines[:1])
        table[chunk, some : 2 * some] = np.kron(eye, sines[-1:])
    table[0, 2 * some :, :span] = sines
    table[-1, 2 * some :, -span:] = sines
    return split_table(table)


def halves(values):
    high = values.astype(jnp.bfloat16)
    low = (values - high.astype(jnp.float32)).astype(jnp.bfloat16)
    return high, low


def dot3(a, b, dims):
    def one(left, right):
        return lax.dot_general(left, right, (dims, ((), ())), preferred_element_type=jnp.float32)

    return one(a[0], b[0]) + (one(a[0], b[1]) + one(a[1], b[0]))


def swap_bits(tiles):
    tiles = list(tiles)
    lanes = tiles[0].shape[1]
    lane = lax.broadcasted_iota(jnp.int32, tiles[0].shape, 1)
    bit = len(tiles) // 2
    while bit:
        upper = (lane & bit) != 0
        for first in range(len(tiles)):
            if first & bit:
                continue
            a, b = tiles[first], tiles[first | bit]
            tiles[first] = jnp.where(upper, pltpu.roll(b, bit, 1), a)
            tiles[first | bit] = jnp.where(upper, b, pltpu.roll(a, lanes - bit, 1))
        bit //= 2
    return tiles


def turn(value, shift):
    lanes = value.shape[1]
    return value if shift % lanes == 0 else pltpu.roll(value, shift % lanes, 1)


def both(values):
    return jnp.concatenate([values, values], axis=0)


def wide(values):
    half = values.shape[1] // 2
    low, high = values[:, :half], values[:, half:]
    return jnp.concatenate([low, low, high, high], axis=1)


def local_forward(place_ref, lower_ref, upper_ref, sigma_ref, rhs_ref, stream_ref, sine_ref, edge_ref, rows_ref, inv_ref, send_ref, sol_ref, edges_ref):
    rows, span, nx_len = rows_ref.shape
    some = rhs_ref.shape[0]
    half = nx_len // 2
    index = pl.program_id(0)
    steps = rows // some
    field = rhs_ref[...].reshape(some * span, nx_len)
    first, second = field[:, :half], field[:, half:]
    parts = []
    for parity, folded in enumerate((first + second, first - second)):
        parts.append(dot3(halves(folded), (stream_ref[0, parity], stream_ref[1, parity]), ((1,), (0,))))
    lane = lax.broadcasted_iota(jnp.int32, (1, nx_len), 1)
    scale = jnp.where(lane == 0, 1.0 / nx_len, 2.0 / nx_len)
    modes = jnp.concatenate(parts, axis=1) * scale
    modes = dot3((sine_ref[0], sine_ref[1]), halves(modes), ((1,), (0,)))
    rows_ref[pl.ds(index * some, some)] = modes.reshape(some, span, nx_len)

    @pl.when(index == steps - 1)
    def _():
        base = place_ref[1] * rows
        sigma = sigma_ref[...]
        step = 8

        def descend(chunk, carry):
            value, numer, denom = carry
            for k in range(step):
                row = chunk * step + k
                low, high = lower_ref[base + row], upper_ref[base + row]
                numer = low * numer + sigma * denom
                new = numer + high * denom
                inv = denom / new
                denom = new
                inv_ref[row] = inv
                value = (low * value - rows_ref[row]) * wide(inv)
                sol_ref[row] = value
            return value, numer, denom

        one = jnp.ones_like(sigma)
        zero = jnp.zeros((span, nx_len), jnp.float32)
        lax.fori_loop(0, rows // step, descend, (zero, one, one))

        def ascend(chunk, value):
            for k in range(step):
                row = rows - 1 - (chunk * step + k)
                value = sol_ref[row] + wide(upper_ref[base + row] * inv_ref[row]) * value
                sol_ref[row] = value
            return value

        lax.fori_loop(0, rows // step, ascend, zero)
        for chunk in range(steps):
            part = sol_ref[chunk * some : chunk * some + some].reshape(some * span, nx_len)
            edges = dot3((edge_ref[0, chunk], edge_ref[1, chunk]), halves(part), ((1,), (0,)))
            edges_ref[chunk * some : chunk * some + some] = edges[:some]
            edges_ref[rows + chunk * some : rows + chunk * some + some] = edges[some : 2 * some]
            if chunk == 0:
                edges_ref[2 * rows : 2 * rows + span] = edges[2 * some :]
            if chunk == steps - 1:
                edges_ref[2 * rows + span :] = edges[2 * some :]
        groups, both_parts, _ = send_ref.shape
        count = both_parts // 2
        quarter = nx_len // 4
        for tile in range(4):
            turned = edges_ref[:, tile * quarter : tile * quarter + quarter].T
            place = tile // 2 * (groups // 2)
            part = tile % 2 * count
            send_ref[place : place + groups // 2, part : part + count] = turned.reshape(groups // 2, count, -1)


def local_inverse(place_ref, lower_ref, upper_ref, piece_ref, rows_ref, inv_ref, weight_ref, stream_ref, sine_ref, out_ref, sol_ref, edges_ref):
    rows, span, nx_len = rows_ref.shape
    some = out_ref.shape[0]
    half = nx_len // 2
    index = pl.program_id(0)

    @pl.when(index == 0)
    def _():
        base = place_ref[1] * rows
        groups, both_parts, _ = piece_ref.shape
        count = both_parts // 2
        quarter = nx_len // 4
        for tile in range(4):
            place = tile // 2 * (groups // 2)
            part = tile % 2 * count
            block = piece_ref[place : place + groups // 2, part : part + count]
            edges_ref[:, tile * quarter : tile * quarter + quarter] = block.reshape(quarter, -1).T
        sines = (sine_ref[0, :span, :span], sine_ref[1, :span, :span])
        before = dot3(sines, halves(edges_ref[2 * rows : 2 * rows + span]), ((1,), (0,)))
        after = dot3(sines, halves(edges_ref[2 * rows + span :]), ((1,), (0,)))
        weight_low, weight_high = weight_ref[0], weight_ref[1]
        step = 8

        def descend(chunk, value):
            for k in range(step):
                row = chunk * step + k
                source = rows_ref[row] - weight_low * edges_ref[pl.ds(row, 1)] - weight_high * edges_ref[pl.ds(rows + row, 1)]
                value = (lower_ref[base + row] * value - source) * wide(inv_ref[row])
                sol_ref[row] = value
            return value

        lax.fori_loop(0, rows // step, descend, before)

        def ascend(chunk, value):
            for k in range(step):
                row = rows - 1 - (chunk * step + k)
                value = sol_ref[row] + wide(upper_ref[base + row] * inv_ref[row]) * value
                sol_ref[row] = value
            return value

        lax.fori_loop(0, rows // step, ascend, after)

    modes = sol_ref[pl.ds(index * some, some)].reshape(some * span, nx_len)
    field = dot3((sine_ref[0], sine_ref[1]), halves(modes), ((1,), (0,))) * (2.0 / (span + 1))
    outs = []
    for parity in range(2):
        part = field[:, parity * half : parity * half + half]
        outs.append(dot3(halves(part), (stream_ref[0, parity], stream_ref[1, parity]), ((1,), (1,))))
    even, odd = outs
    out_ref[:, :, :half] = (even + odd).reshape(some, span, half)
    out_ref[:, :, half:] = (even - odd).reshape(some, span, half)


def factor(place_ref, lower_ref, upper_ref, waves_ref, both_ref, carry_down_ref, carry_up_ref, close_ref, start_ref):
    rows = both_ref.shape[1]
    blocks = carry_down_ref.shape[0]
    total = rows * blocks
    sigma = waves_ref[...]
    one = jnp.ones_like(sigma)
    step = 8

    def step_down(row, numer, denom):
        numer = lower_ref[row] * numer + sigma * denom
        return numer, numer + upper_ref[row] * denom

    def step_up(row, numer, denom):
        numer = upper_ref[row] * numer + sigma * denom
        return numer, numer + lower_ref[row] * denom

    def block(index, carry):
        t_down, t_up = carry
        other = blocks - 1 - index
        start_ref[0, index] = t_down
        start_ref[1, other] = t_up

        def some(chunk, inner):
            nd, dd, nu, du, prod_l, prod_u = inner
            for k in range(step):
                row = index * rows + chunk * step + k
                back = total - 1 - row
                nd, dd = step_down(row, nd, dd)
                nu, du = step_up(back, nu, du)
                prod_l = prod_l * lower_ref[row]
                prod_u = prod_u * upper_ref[back]
            return nd, dd, nu, du, prod_l, prod_u

        unit = jnp.float32(1.0)
        nd, dd, nu, du, prod_l, prod_u = lax.fori_loop(
            0, rows // step, some, (t_down, one, t_up, one, unit, unit)
        )
        inv_d = 1.0 / dd
        inv_u = 1.0 / du
        carry_down_ref[index] = prod_l * inv_d
        carry_up_ref[other] = prod_u * inv_u
        return nd * inv_d, nu * inv_u

    lax.fori_loop(0, blocks, block, (one, one))
    place = place_ref[1]
    first = place * rows

    def own(chunk, inner):
        nd, dd, nu, du = inner
        for k in range(step):
            row = chunk * step + k
            back = rows - 1 - row
            nd, new_d = step_down(first + row, nd, dd)
            both_ref[0, row] = dd / new_d
            nu, new_u = step_up(first + back, nu, du)
            both_ref[1, back] = du / new_u
            dd, du = new_d, new_u
        return nd, dd, nu, du

    nd, dd, nu, du = lax.fori_loop(
        0, rows // step, own, (start_ref[0, place], one, start_ref[1, place], one)
    )
    t_end = nd / dd
    t_next = start_ref[1, place]
    is_last = place == blocks - 1
    inner = jnp.where(is_last, 0.0, 1.0 / (t_next + t_end * (1.0 - t_next)))
    close_ref[0] = inner
    close_ref[1] = inner * (1.0 - t_next)
    close_ref[2] = 1.0 - start_ref[0, place]
    close_ref[3] = 1.0 - t_next


def span_forward(place_ref, lower_ref, upper_ref, piece_ref, factor_ref, close_ref, plane_ref, cell_ref, rows_ref, send_ref, keep_ref, edge_ref):
    groups, parts, lanes = piece_ref.shape
    rows, _, nz_len = rows_ref.shape
    span = nz_len // groups
    per = lanes // groups
    tiles = swap_bits([piece_ref[t] for t in range(groups)])
    lane = lax.broadcasted_iota(jnp.int32, (parts, lanes), 1)

    def source(value, group):
        return turn(tiles[value % groups], groups * (group - value // groups))

    for row in range(rows):
        pair = jnp.where(lane < groups, source(row, 0), source(rows + row, 1))
        keep_ref[row] = jnp.where(lane < 2 * groups, pair, 0.0)
    wave = lax.broadcasted_iota(jnp.int32, (1, nz_len), 1)
    scale = jnp.where(wave % (nz_len // 2) == 0, 1.0 / nz_len, 2.0 / nz_len)
    planes = keep_ref[...].reshape(rows * parts, lanes)
    spec = dot3(halves(planes), (plane_ref[0], plane_ref[1]), ((1,), (0,)))
    rows_ref[...] = (spec * (-span_weight * scale)).reshape(rows, parts, nz_len)
    cells = []
    for side in range(2):
        built = []
        for tile in range(nz_len // lanes):
            value = source(2 * rows + side * span + tile * per, 0)
            for group in range(1, per):
                other = source(2 * rows + side * span + tile * per + group, group)
                value = jnp.where(lane < groups * group, value, other)
            built.append(value)
        cells.append(jnp.concatenate(built, axis=1))
    edges = dot3(halves(jnp.concatenate(cells, axis=0)), (cell_ref[0], cell_ref[1]), ((1,), (0,))) * scale
    low_edge, high_edge = edges[:parts], edges[parts:]
    edge_ref[0] = low_edge
    edge_ref[1] = high_edge
    base = place_ref[1] * rows
    step = 8

    def sweep(chunk, carry):
        down, up = carry
        for k in range(step):
            row = chunk * step + k
            back = rows - 1 - row
            down = (lower_ref[base + row] * down - rows_ref[row]) * both(factor_ref[0, row])
            up = (upper_ref[base + back] * up - rows_ref[back]) * both(factor_ref[1, back])
        return down, up

    start = (both(close_ref[2]) * low_edge, both(close_ref[3]) * high_edge)
    down, up = lax.fori_loop(0, rows // step, sweep, start)
    down = down + high_edge
    up = up + low_edge
    for target in range(send_ref.shape[0]):
        send_ref[target] = jnp.where(target > place_ref[1], down, up)


def span_inverse(place_ref, lower_ref, upper_ref, rows_ref, ends_ref, keep_ref, edge_ref, factor_ref, carry_down_ref, carry_up_ref, close_ref, plane_ref, cell_ref, out_ref, grow_ref, near_ref):
    groups, parts, lanes = out_ref.shape
    rows, _, nz_len = rows_ref.shape
    blocks = ends_ref.shape[0]
    span = nz_len // groups
    per = lanes // groups
    place = place_ref[1]
    base = place * rows
    step = 8
    zero = jnp.zeros((parts, nz_len), jnp.float32)
    before = lax.fori_loop(
        0, place, lambda k, value: ends_ref[k] + both(carry_down_ref[k]) * value, zero
    )

    def climb(k, value):
        other = blocks - 1 - k
        return ends_ref[other] + both(carry_up_ref[other]) * value

    after = lax.fori_loop(0, blocks - 1 - place, climb, zero)
    before = before + both(close_ref[2]) * edge_ref[0]
    after = after + both(close_ref[3]) * edge_ref[1]

    def descend(chunk, value):
        for k in range(step):
            row = chunk * step + k
            value = (lower_ref[base + row] * value - rows_ref[row]) * both(factor_ref[0, row])
            grow_ref[row] = value
        return value

    last = lax.fori_loop(0, rows // step, descend, before)
    beyond = both(close_ref[0]) * after + both(close_ref[1]) * last

    def ascend(chunk, value):
        for k in range(step):
            row = rows - 1 - (chunk * step + k)
            ratio = upper_ref[base + row] * factor_ref[0, row]
            value = grow_ref[row] + both(ratio) * value
            grow_ref[row] = value
        return value

    first = lax.fori_loop(0, rows // step, ascend, beyond)
    below = before + both(close_ref[2]) * first
    flat = grow_ref[...].reshape(rows * parts, nz_len)
    near = dot3(halves(flat), (plane_ref[0], plane_ref[1]), ((1,), (1,)))
    near_ref[...] = near.reshape(rows, parts, lanes)
    edges = jnp.concatenate([below, beyond], axis=0)
    cells = dot3(halves(edges), (cell_ref[0], cell_ref[1]), ((1,), (1,)))
    lane = lax.broadcasted_iota(jnp.int32, (parts, lanes), 1)
    total = []
    for row in range(rows):
        own = keep_ref[row]
        left = jnp.where(lane == 0, turn(own, 1 - 2 * groups), turn(own, 1 - groups))
        right = jnp.where(lane == 2 * groups - 1, turn(own, 2 * groups - 1), turn(own, groups - 1))
        total.append(near_ref[row] + jnp.where(lane < groups, left, right))

    def piece(value, group):
        if value < rows:
            return turn(total[value], groups * group)
        if value < 2 * rows:
            return turn(total[value - rows], groups * (group - 1))
        side, cell = divmod(value - 2 * rows, span)
        tile, part = divmod(cell, per)
        found = cells[side * parts : side * parts + parts, tile * lanes : tile * lanes + lanes]
        return turn(found, groups * (group - part))

    tiles = []
    for t in range(groups):
        value = piece(t, 0)
        for group in range(1, per):
            value = jnp.where(lane < groups * group, value, piece(groups * group + t, group))
        tiles.append(value)
    for t, value in enumerate(swap_bits(tiles)):
        out_ref[t] = value


smem = pl.BlockSpec(memory_space=pltpu.SMEM)
vmem = pl.BlockSpec(memory_space=pltpu.VMEM)


def local(rhs, lower, upper):
    rows, span, nx_len = rhs.shape
    groups = lax.axis_size("row")
    blocks = lax.axis_size("col")
    nz_len = span * groups
    modes = nx_len // 2 // groups
    parts = 2 * modes
    steps = 3
    some = rows // steps
    lanes = 2 * (rows + span)
    place = jnp.stack([lax.axis_index("row"), lax.axis_index("col")]).astype(jnp.int32)
    f32 = jnp.float32
    params = pltpu.CompilerParams(vmem_limit_bytes=40 * 1024 * 1024)
    stream = stream_table(nx_len)
    sines = split_table(np.kron(np.eye(some), sine_matrix(span)))
    edge = edge_table(span, some, steps)
    plane = plane_table(nz_len, groups)
    plane = jnp.pad(plane, ((0, 0), (0, lanes - 2 * groups), (0, 0)))
    cell = cell_table(nz_len, groups)
    ends_of_block = sine_matrix(span)[[0, -1]] * span_weight
    weights = jnp.asarray(np.broadcast_to(ends_of_block[:, :, None], (2, span, nx_len)).astype(np.float32))

    def on_chip(*shape):
        return pltpu.VMEM(shape, f32)

    def on_hbm(value):
        return pltpu.with_memory_space_constraint(value, pltpu.HBM)

    def exchange(value, axis):
        return lax.all_to_all(value, axis, split_axis=0, concat_axis=0, tiled=True)

    def stream_part(index):
        angle = 2.0 * math.pi / nx_len * index.astype(f32)
        return stream_weight * (2.0 - 2.0 * jnp.cos(angle))

    def span_part(index, count):
        angle = 2.0 * math.pi / count * index.astype(f32)
        return span_weight * (2.0 - 2.0 * jnp.cos(angle))

    quarter = nx_len // 4
    every = jnp.arange(nx_len // 2)
    kx = 2 * (every % quarter) + every // quarter
    kz = span_part(jnp.arange(1, span + 1), 2 * (span + 1))
    sigma_own = kz[:, None] + stream_part(kx)[None, :] + shift_value
    field_spec = pl.BlockSpec((some, span, nx_len), lambda i: (i, 0, 0))
    own_rows, own_inv, send = pl.pallas_call(
        local_forward,
        grid=(steps,),
        in_specs=[smem, smem, smem, vmem, field_spec, vmem, vmem, vmem],
        out_specs=[vmem] * 3,
        out_shape=[on_chip(rows, span, nx_len), on_chip(rows, span, nx_len // 2), on_chip(groups, parts, lanes)],
        scratch_shapes=[on_chip(rows, span, nx_len), on_chip(lanes, nx_len)],
        compiler_params=params,
        name="local_forward",
    )(place, lower, upper, sigma_own, on_hbm(rhs), stream, sines, edge)
    piece = exchange(send, "row")

    order = place[0] * modes + jnp.arange(modes)
    kx = 2 * (order % quarter) + order // quarter
    kz = jnp.asarray(span_waves(nz_len).astype(np.int32))
    sigma = stream_part(kx)[:, None] + span_part(kz, nz_len)[None, :] + shift_value
    factors, carry_down, carry_up, close = pl.pallas_call(
        factor,
        in_specs=[smem, smem, smem, vmem],
        out_specs=[vmem] * 4,
        out_shape=[
            on_chip(2, rows, modes, nz_len),
            on_chip(blocks, modes, nz_len),
            on_chip(blocks, modes, nz_len),
            on_chip(4, modes, nz_len),
        ],
        scratch_shapes=[on_chip(2, blocks, modes, nz_len)],
        compiler_params=params,
        name="factor",
    )(place, lower, upper, sigma)

    mode_rows, ends, keep, edges = pl.pallas_call(
        span_forward,
        in_specs=[smem, smem, smem] + [vmem] * 5,
        out_specs=[vmem] * 4,
        out_shape=[
            on_chip(rows, parts, nz_len),
            on_chip(blocks, parts, nz_len),
            on_chip(rows, parts, lanes),
            on_chip(2, parts, nz_len),
        ],
        compiler_params=params,
        name="span_forward",
    )(place, lower, upper, piece, factors, close, plane, cell)
    ends = exchange(ends, "col")

    send = pl.pallas_call(
        span_inverse,
        in_specs=[smem, smem, smem] + [vmem] * 10,
        out_specs=vmem,
        out_shape=on_chip(groups, parts, lanes),
        scratch_shapes=[on_chip(rows, parts, nz_len), on_chip(rows, parts, lanes)],
        compiler_params=params,
        name="span_inverse",
    )(place, lower, upper, mode_rows, ends, keep, edges, factors, carry_down, carry_up, close, plane, cell)
    piece = exchange(send, "row")

    return pl.pallas_call(
        local_inverse,
        grid=(steps,),
        in_specs=[smem, smem, smem] + [vmem] * 6,
        out_specs=field_spec,
        out_shape=jax.ShapeDtypeStruct((rows, span, nx_len), f32),
        scratch_shapes=[on_chip(rows, span, nx_len), on_chip(lanes, nx_len)],
        compiler_params=params,
        name="local_inverse",
    )(place, lower, upper, piece, own_rows, own_inv, weights, stream, sines)


def solution(mesh):
    return jax.shard_map(
        local,
        mesh=mesh,
        in_specs=(P("col", "row", None), P(), P()),
        out_specs=P("col", "row", None),
        check_vma=False,
    )
```

```python
import math

import jax
import jax.numpy as jnp
import ml_dtypes
import numpy as np
from jax import lax
from jax.experimental import pallas as pl
from jax.experimental.pallas import tpu as pltpu
from jax.sharding import PartitionSpec as P

stream_weight = 0.04
span_weight = 0.16
shift_value = 0.0002


def split_table(values):
    high = values.astype(ml_dtypes.bfloat16)
    low = (values - high.astype(np.float64)).astype(ml_dtypes.bfloat16)
    return jnp.asarray(np.stack([high, low]))


def stream_table(nx_len):
    half = nx_len // 2
    wave = 2 * np.arange(half // 2)[None, None, :] + np.arange(2)[:, None, None]
    angle = 2.0 * math.pi / nx_len * (np.arange(half)[None, :, None] * wave % nx_len)
    return split_table(np.concatenate([np.cos(angle), -np.sin(angle)], axis=2))


def span_waves(nz_len):
    half = nz_len // 2
    wave = np.arange(half)
    return np.concatenate([wave, np.where(wave == 0, half, wave)])


def span_basis(points, nz_len):
    angle = 2.0 * math.pi / nz_len * (points[:, None] * span_waves(nz_len)[None, :] % nz_len)
    cosine = np.arange(nz_len)[None, :] <= nz_len // 2
    return np.where(cosine, np.cos(angle), np.sin(angle))


def plane_table(nz_len, groups):
    span = nz_len // groups
    block = np.arange(groups) * span
    return split_table(span_basis(np.concatenate([block - 1, block + span]) % nz_len, nz_len))


def cell_table(nz_len, groups):
    return split_table(span_basis(np.arange(nz_len).reshape(groups, -1).T.reshape(-1), nz_len))


def sine_matrix(span):
    index = np.arange(1, span + 1)
    return np.sin(math.pi / (span + 1) * index[:, None] * index[None, :])


def halves(values):
    high = values.astype(jnp.bfloat16)
    low = (values - high.astype(jnp.float32)).astype(jnp.bfloat16)
    return high, low


def dot3(a, b, dims):
    def one(left, right):
        return lax.dot_general(left, right, (dims, ((), ())), preferred_element_type=jnp.float32)

    return one(a[0], b[0]) + (one(a[0], b[1]) + one(a[1], b[0]))


def swap_bits(tiles):
    tiles = list(tiles)
    lanes = tiles[0].shape[1]
    lane = lax.broadcasted_iota(jnp.int32, tiles[0].shape, 1)
    bit = len(tiles) // 2
    while bit:
        upper = (lane & bit) != 0
        for first in range(len(tiles)):
            if first & bit:
                continue
            a, b = tiles[first], tiles[first | bit]
            tiles[first] = jnp.where(upper, pltpu.roll(b, bit, 1), a)
            tiles[first | bit] = jnp.where(upper, b, pltpu.roll(a, lanes - bit, 1))
        bit //= 2
    return tiles


def turn(value, shift):
    lanes = value.shape[1]
    return value if shift % lanes == 0 else pltpu.roll(value, shift % lanes, 1)


def both(values):
    return jnp.concatenate([values, values], axis=0)


def wide(values):
    half = values.shape[1] // 2
    low, high = values[:, :half], values[:, half:]
    return jnp.concatenate([low, low, high, high], axis=1)


def local_forward(place_ref, lower_ref, upper_ref, sigma_ref, weight_ref, rhs_ref, stream_ref, sine_ref, rows_ref, inv_ref, send_ref, sol_ref, ratio_ref, value_ref, state_ref, edges_ref):
    some, span, nx_len = rows_ref.shape
    rows = sol_ref.shape[0]
    half = nx_len // 2
    index = pl.program_id(0)
    steps = rows // some

    @pl.when(index == 0)
    def _():
        value_ref[...] = jnp.zeros_like(value_ref)
        state_ref[...] = jnp.ones_like(state_ref)

    field = rhs_ref[...].reshape(some * span, nx_len)
    first, second = field[:, :half], field[:, half:]
    parts = []
    for parity, folded in enumerate((first + second, first - second)):
        parts.append(dot3(halves(folded), (stream_ref[0, parity], stream_ref[1, parity]), ((1,), (0,))))
    lane = lax.broadcasted_iota(jnp.int32, (1, nx_len), 1)
    scale = jnp.where(lane == 0, 1.0 / nx_len, 2.0 / nx_len)
    modes = jnp.concatenate(parts, axis=1) * scale
    modes = dot3((sine_ref[0], sine_ref[1]), halves(modes), ((1,), (0,)))
    rows_ref[...] = modes.reshape(some, span, nx_len)
    base = place_ref[1] * rows
    sigma = sigma_ref[...]
    step = 8

    def descend(chunk, carry):
        value, numer, denom = carry
        for k in range(step):
            row = chunk * step + k
            cell = index * some + row
            low, high = lower_ref[base + cell], upper_ref[base + cell]
            numer = low * numer + sigma * denom
            new = numer + high * denom
            inv = denom / new
            denom = new
            inv_ref[row] = inv
            ratio_ref[cell] = high * inv
            value = (low * value - rows_ref[row]) * wide(inv)
            sol_ref[cell] = value
        return value, numer, denom

    value, numer, denom = lax.fori_loop(
        0, some // step, descend, (value_ref[...], state_ref[0], state_ref[1])
    )
    value_ref[...] = value
    state_ref[0] = numer
    state_ref[1] = denom

    @pl.when(index == steps - 1)
    def _():
        weight = weight_ref[0] * (2.0 / ((span + 1) * span_weight))
        flip = lax.broadcasted_iota(jnp.int32, (span // 2, nx_len), 0) % 2 == 0

        def ascend(chunk, value):
            for k in range(step):
                row = rows - 1 - (chunk * step + k)
                value = sol_ref[row] + wide(ratio_ref[row]) * value
                sol_ref[row] = value
                part = weight * value
                part = part[: span // 2] + part[span // 2 :]
                edges_ref[pl.ds(row, 1)] = jnp.sum(part, axis=0, keepdims=True)
                part = jnp.where(flip, part, -part)
                edges_ref[pl.ds(rows + row, 1)] = jnp.sum(part, axis=0, keepdims=True)
            return value

        lax.fori_loop(0, rows // step, ascend, jnp.zeros((span, nx_len), jnp.float32))
        sines = (sine_ref[0, :span, :span], sine_ref[1, :span, :span])
        for side, row in enumerate((0, rows - 1)):
            edge = dot3(sines, halves(sol_ref[row]), ((1,), (0,))) * (2.0 / (span + 1))
            edges_ref[2 * rows + side * span : 2 * rows + side * span + span] = edge
        groups, both_parts, _ = send_ref.shape
        count = both_parts // 2
        quarter = nx_len // 4
        for tile in range(4):
            turned = edges_ref[:, tile * quarter : tile * quarter + quarter].T
            place = tile // 2 * (groups // 2)
            part = tile % 2 * count
            send_ref[place : place + groups // 2, part : part + count] = turned.reshape(groups // 2, count, -1)


def local_inverse(place_ref, lower_ref, upper_ref, piece_ref, rows_ref, inv_ref, weight_ref, stream_ref, sine_ref, out_ref, sol_ref, edges_ref):
    rows, span, nx_len = rows_ref.shape
    some = out_ref.shape[0]
    half = nx_len // 2
    index = pl.program_id(0)

    @pl.when(index == 0)
    def _():
        base = place_ref[1] * rows
        groups, both_parts, _ = piece_ref.shape
        count = both_parts // 2
        quarter = nx_len // 4
        for tile in range(4):
            place = tile // 2 * (groups // 2)
            part = tile % 2 * count
            block = piece_ref[place : place + groups // 2, part : part + count]
            edges_ref[:, tile * quarter : tile * quarter + quarter] = block.reshape(quarter, -1).T
        sines = (sine_ref[0, :span, :span], sine_ref[1, :span, :span])
        before = dot3(sines, halves(edges_ref[2 * rows : 2 * rows + span]), ((1,), (0,)))
        after = dot3(sines, halves(edges_ref[2 * rows + span :]), ((1,), (0,)))
        weight_low, weight_high = weight_ref[0], weight_ref[1]
        step = 8

        def descend(chunk, value):
            for k in range(step):
                row = chunk * step + k
                source = rows_ref[row] - weight_low * edges_ref[pl.ds(row, 1)] - weight_high * edges_ref[pl.ds(rows + row, 1)]
                value = (lower_ref[base + row] * value - source) * wide(inv_ref[row])
                sol_ref[row] = value
            return value

        lax.fori_loop(0, rows // step, descend, before)

        def ascend(chunk, value):
            for k in range(step):
                row = rows - 1 - (chunk * step + k)
                value = sol_ref[row] + wide(upper_ref[base + row] * inv_ref[row]) * value
                sol_ref[row] = value
            return value

        lax.fori_loop(0, rows // step, ascend, after)

    modes = sol_ref[pl.ds(index * some, some)].reshape(some * span, nx_len)
    field = dot3((sine_ref[0], sine_ref[1]), halves(modes), ((1,), (0,))) * (2.0 / (span + 1))
    outs = []
    for parity in range(2):
        part = field[:, parity * half : parity * half + half]
        outs.append(dot3(halves(part), (stream_ref[0, parity], stream_ref[1, parity]), ((1,), (1,))))
    even, odd = outs
    out_ref[:, :, :half] = (even + odd).reshape(some, span, half)
    out_ref[:, :, half:] = (even - odd).reshape(some, span, half)


def factor(place_ref, lower_ref, upper_ref, waves_ref, both_ref, carry_down_ref, carry_up_ref, close_ref, start_ref):
    rows = both_ref.shape[1]
    blocks = carry_down_ref.shape[0]
    total = rows * blocks
    sigma = waves_ref[...]
    one = jnp.ones_like(sigma)
    step = 8

    def step_down(row, numer, denom):
        numer = lower_ref[row] * numer + sigma * denom
        return numer, numer + upper_ref[row] * denom

    def step_up(row, numer, denom):
        numer = upper_ref[row] * numer + sigma * denom
        return numer, numer + lower_ref[row] * denom

    def block(index, carry):
        t_down, t_up = carry
        other = blocks - 1 - index
        start_ref[0, index] = t_down
        start_ref[1, other] = t_up

        def some(chunk, inner):
            nd, dd, nu, du, prod_l, prod_u = inner
            for k in range(step):
                row = index * rows + chunk * step + k
                back = total - 1 - row
                nd, dd = step_down(row, nd, dd)
                nu, du = step_up(back, nu, du)
                prod_l = prod_l * lower_ref[row]
                prod_u = prod_u * upper_ref[back]
            return nd, dd, nu, du, prod_l, prod_u

        unit = jnp.float32(1.0)
        nd, dd, nu, du, prod_l, prod_u = lax.fori_loop(
            0, rows // step, some, (t_down, one, t_up, one, unit, unit)
        )
        inv_d = 1.0 / dd
        inv_u = 1.0 / du
        carry_down_ref[index] = prod_l * inv_d
        carry_up_ref[other] = prod_u * inv_u
        return nd * inv_d, nu * inv_u

    lax.fori_loop(0, blocks, block, (one, one))
    place = place_ref[1]
    first = place * rows

    def own(chunk, inner):
        nd, dd, nu, du = inner
        for k in range(step):
            row = chunk * step + k
            back = rows - 1 - row
            nd, new_d = step_down(first + row, nd, dd)
            both_ref[0, row] = dd / new_d
            nu, new_u = step_up(first + back, nu, du)
            both_ref[1, back] = du / new_u
            dd, du = new_d, new_u
        return nd, dd, nu, du

    nd, dd, nu, du = lax.fori_loop(
        0, rows // step, own, (start_ref[0, place], one, start_ref[1, place], one)
    )
    t_end = nd / dd
    t_next = start_ref[1, place]
    is_last = place == blocks - 1
    inner = jnp.where(is_last, 0.0, 1.0 / (t_next + t_end * (1.0 - t_next)))
    close_ref[0] = inner
    close_ref[1] = inner * (1.0 - t_next)
    close_ref[2] = 1.0 - start_ref[0, place]
    close_ref[3] = 1.0 - t_next


def span_forward(place_ref, lower_ref, upper_ref, piece_ref, factor_ref, close_ref, plane_ref, cell_ref, rows_ref, send_ref, keep_ref, edge_ref):
    groups, parts, lanes = piece_ref.shape
    rows, _, nz_len = rows_ref.shape
    span = nz_len // groups
    per = lanes // groups
    tiles = swap_bits([piece_ref[t] for t in range(groups)])
    lane = lax.broadcasted_iota(jnp.int32, (parts, lanes), 1)

    def source(value, group):
        return turn(tiles[value % groups], groups * (group - value // groups))

    for row in range(rows):
        pair = jnp.where(lane < groups, source(row, 0), source(rows + row, 1))
        keep_ref[row] = jnp.where(lane < 2 * groups, pair, 0.0)
    wave = lax.broadcasted_iota(jnp.int32, (1, nz_len), 1)
    scale = jnp.where(wave % (nz_len // 2) == 0, 1.0 / nz_len, 2.0 / nz_len)
    planes = keep_ref[...].reshape(rows * parts, lanes)
    spec = dot3(halves(planes), (plane_ref[0], plane_ref[1]), ((1,), (0,)))
    rows_ref[...] = (spec * (-span_weight * scale)).reshape(rows, parts, nz_len)
    cells = []
    for side in range(2):
        built = []
        for tile in range(nz_len // lanes):
            value = source(2 * rows + side * span + tile * per, 0)
            for group in range(1, per):
                other = source(2 * rows + side * span + tile * per + group, group)
                value = jnp.where(lane < groups * group, value, other)
            built.append(value)
        cells.append(jnp.concatenate(built, axis=1))
    edges = dot3(halves(jnp.concatenate(cells, axis=0)), (cell_ref[0], cell_ref[1]), ((1,), (0,))) * scale
    low_edge, high_edge = edges[:parts], edges[parts:]
    edge_ref[0] = low_edge
    edge_ref[1] = high_edge
    base = place_ref[1] * rows
    step = 8

    def sweep(chunk, carry):
        down, up = carry
        for k in range(step):
            row = chunk * step + k
            back = rows - 1 - row
            down = (lower_ref[base + row] * down - rows_ref[row]) * both(factor_ref[0, row])
            up = (upper_ref[base + back] * up - rows_ref[back]) * both(factor_ref[1, back])
        return down, up

    start = (both(close_ref[2]) * low_edge, both(close_ref[3]) * high_edge)
    down, up = lax.fori_loop(0, rows // step, sweep, start)
    down = down + high_edge
    up = up + low_edge
    for target in range(send_ref.shape[0]):
        send_ref[target] = jnp.where(target > place_ref[1], down, up)


def span_inverse(place_ref, lower_ref, upper_ref, rows_ref, ends_ref, keep_ref, edge_ref, factor_ref, carry_down_ref, carry_up_ref, close_ref, plane_ref, cell_ref, out_ref, grow_ref, near_ref):
    groups, parts, lanes = out_ref.shape
    rows, _, nz_len = rows_ref.shape
    blocks = ends_ref.shape[0]
    span = nz_len // groups
    per = lanes // groups
    place = place_ref[1]
    base = place * rows
    step = 8
    zero = jnp.zeros((parts, nz_len), jnp.float32)
    before = lax.fori_loop(
        0, place, lambda k, value: ends_ref[k] + both(carry_down_ref[k]) * value, zero
    )

    def climb(k, value):
        other = blocks - 1 - k
        return ends_ref[other] + both(carry_up_ref[other]) * value

    after = lax.fori_loop(0, blocks - 1 - place, climb, zero)
    before = before + both(close_ref[2]) * edge_ref[0]
    after = after + both(close_ref[3]) * edge_ref[1]

    def descend(chunk, value):
        for k in range(step):
            row = chunk * step + k
            value = (lower_ref[base + row] * value - rows_ref[row]) * both(factor_ref[0, row])
            grow_ref[row] = value
        return value

    last = lax.fori_loop(0, rows // step, descend, before)
    beyond = both(close_ref[0]) * after + both(close_ref[1]) * last

    def ascend(chunk, value):
        for k in range(step):
            row = rows - 1 - (chunk * step + k)
            ratio = upper_ref[base + row] * factor_ref[0, row]
            value = grow_ref[row] + both(ratio) * value
            grow_ref[row] = value
        return value

    first = lax.fori_loop(0, rows // step, ascend, beyond)
    below = before + both(close_ref[2]) * first
    flat = grow_ref[...].reshape(rows * parts, nz_len)
    near = dot3(halves(flat), (plane_ref[0], plane_ref[1]), ((1,), (1,)))
    near_ref[...] = near.reshape(rows, parts, lanes)
    edges = jnp.concatenate([below, beyond], axis=0)
    cells = dot3(halves(edges), (cell_ref[0], cell_ref[1]), ((1,), (1,)))
    lane = lax.broadcasted_iota(jnp.int32, (parts, lanes), 1)
    total = []
    for row in range(rows):
        own = keep_ref[row]
        left = jnp.where(lane == 0, turn(own, 1 - 2 * groups), turn(own, 1 - groups))
        right = jnp.where(lane == 2 * groups - 1, turn(own, 2 * groups - 1), turn(own, groups - 1))
        total.append(near_ref[row] + jnp.where(lane < groups, left, right))

    def piece(value, group):
        if value < rows:
            return turn(total[value], groups * group)
        if value < 2 * rows:
            return turn(total[value - rows], groups * (group - 1))
        side, cell = divmod(value - 2 * rows, span)
        tile, part = divmod(cell, per)
        found = cells[side * parts : side * parts + parts, tile * lanes : tile * lanes + lanes]
        return turn(found, groups * (group - part))

    tiles = []
    for t in range(groups):
        value = piece(t, 0)
        for group in range(1, per):
            value = jnp.where(lane < groups * group, value, piece(groups * group + t, group))
        tiles.append(value)
    for t, value in enumerate(swap_bits(tiles)):
        out_ref[t] = value


smem = pl.BlockSpec(memory_space=pltpu.SMEM)
vmem = pl.BlockSpec(memory_space=pltpu.VMEM)


def local(rhs, lower, upper):
    rows, span, nx_len = rhs.shape
    groups = lax.axis_size("row")
    blocks = lax.axis_size("col")
    nz_len = span * groups
    modes = nx_len // 2 // groups
    parts = 2 * modes
    steps = 3
    some = rows // steps
    lanes = 2 * (rows + span)
    place = jnp.stack([lax.axis_index("row"), lax.axis_index("col")]).astype(jnp.int32)
    f32 = jnp.float32
    params = pltpu.CompilerParams(vmem_limit_bytes=40 * 1024 * 1024)
    stream = stream_table(nx_len)
    sines = split_table(np.kron(np.eye(some), sine_matrix(span)))
    plane = plane_table(nz_len, groups)
    plane = jnp.pad(plane, ((0, 0), (0, lanes - 2 * groups), (0, 0)))
    cell = cell_table(nz_len, groups)
    ends_of_block = sine_matrix(span)[[0, -1]] * span_weight
    weights = jnp.asarray(np.broadcast_to(ends_of_block[:, :, None], (2, span, nx_len)).astype(np.float32))

    def on_chip(*shape):
        return pltpu.VMEM(shape, f32)

    def on_hbm(value):
        return pltpu.with_memory_space_constraint(value, pltpu.HBM)

    def fixed(value):
        shape = value.shape
        return pl.BlockSpec(shape, lambda i: (0,) * len(shape))

    def exchange(value, axis):
        return lax.all_to_all(value, axis, split_axis=0, concat_axis=0, tiled=True)

    def stream_part(index):
        angle = 2.0 * math.pi / nx_len * index.astype(f32)
        return stream_weight * (2.0 - 2.0 * jnp.cos(angle))

    def span_part(index, count):
        angle = 2.0 * math.pi / count * index.astype(f32)
        return span_weight * (2.0 - 2.0 * jnp.cos(angle))

    quarter = nx_len // 4
    every = jnp.arange(nx_len // 2)
    kx = 2 * (every % quarter) + every // quarter
    kz = span_part(jnp.arange(1, span + 1), 2 * (span + 1))
    sigma_own = kz[:, None] + stream_part(kx)[None, :] + shift_value
    field_spec = pl.BlockSpec((some, span, nx_len), lambda i: (i, 0, 0))
    mode_spec = pl.BlockSpec((some, span, nx_len), lambda i: (i, 0, 0))
    inv_spec = pl.BlockSpec((some, span, nx_len // 2), lambda i: (i, 0, 0))
    own_rows, own_inv, send = pl.pallas_call(
        local_forward,
        grid=(steps,),
        in_specs=[smem, smem, smem, vmem, fixed(weights), field_spec, fixed(stream), fixed(sines)],
        out_specs=[mode_spec, inv_spec, vmem],
        out_shape=[
            pltpu.HBM((rows, span, nx_len), f32),
            pltpu.HBM((rows, span, nx_len // 2), f32),
            on_chip(groups, parts, lanes),
        ],
        scratch_shapes=[
            on_chip(rows, span, nx_len),
            on_chip(rows, span, nx_len // 2),
            on_chip(span, nx_len),
            on_chip(2, span, nx_len // 2),
            on_chip(lanes, nx_len),
        ],
        compiler_params=params,
        name="local_forward",
    )(place, on_hbm(lower), on_hbm(upper), sigma_own, on_hbm(weights), on_hbm(rhs), on_hbm(stream), on_hbm(sines))
    piece = exchange(send, "row")

    order = place[0] * modes + jnp.arange(modes)
    kx = 2 * (order % quarter) + order // quarter
    kz = jnp.asarray(span_waves(nz_len).astype(np.int32))
    sigma = stream_part(kx)[:, None] + span_part(kz, nz_len)[None, :] + shift_value
    factors, carry_down, carry_up, close = pl.pallas_call(
        factor,
        in_specs=[smem, smem, smem, vmem],
        out_specs=[vmem] * 4,
        out_shape=[
            on_chip(2, rows, modes, nz_len),
            on_chip(blocks, modes, nz_len),
            on_chip(blocks, modes, nz_len),
            on_chip(4, modes, nz_len),
        ],
        scratch_shapes=[on_chip(2, blocks, modes, nz_len)],
        compiler_params=params,
        name="factor",
    )(place, lower, upper, sigma)

    mode_rows, ends, keep, edges = pl.pallas_call(
        span_forward,
        in_specs=[smem, smem, smem] + [vmem] * 5,
        out_specs=[vmem] * 4,
        out_shape=[
            on_chip(rows, parts, nz_len),
            on_chip(blocks, parts, nz_len),
            on_chip(rows, parts, lanes),
            on_chip(2, parts, nz_len),
        ],
        compiler_params=params,
        name="span_forward",
    )(place, lower, upper, piece, factors, close, plane, cell)
    ends = exchange(ends, "col")

    send = pl.pallas_call(
        span_inverse,
        in_specs=[smem, smem, smem] + [vmem] * 10,
        out_specs=vmem,
        out_shape=on_chip(groups, parts, lanes),
        scratch_shapes=[on_chip(rows, parts, nz_len), on_chip(rows, parts, lanes)],
        compiler_params=params,
        name="span_inverse",
    )(place, lower, upper, mode_rows, ends, keep, edges, factors, carry_down, carry_up, close, plane, cell)
    piece = exchange(send, "row")

    return pl.pallas_call(
        local_inverse,
        grid=(steps,),
        in_specs=[smem, smem, smem] + [vmem] * 6,
        out_specs=field_spec,
        out_shape=jax.ShapeDtypeStruct((rows, span, nx_len), f32),
        scratch_shapes=[on_chip(rows, span, nx_len), on_chip(lanes, nx_len)],
        compiler_params=params,
        name="local_inverse",
    )(place, lower, upper, piece, own_rows, own_inv, weights, stream, sines)


def solution(mesh):
    return jax.shard_map(
        local,
        mesh=mesh,
        in_specs=(P("col", "row", None), P(), P()),
        out_specs=P("col", "row", None),
        check_vma=False,
    )
```

```python
import math

import jax
import jax.numpy as jnp
import ml_dtypes
import numpy as np
from jax import lax
from jax.experimental import pallas as pl
from jax.experimental.pallas import tpu as pltpu
from jax.sharding import PartitionSpec as P

stream_weight = 0.04
span_weight = 0.16
shift_value = 0.0002


def split_table(values):
    high = values.astype(ml_dtypes.bfloat16)
    low = (values - high.astype(np.float64)).astype(ml_dtypes.bfloat16)
    return jnp.asarray(np.stack([high, low]))


def stream_table(nx_len):
    half = nx_len // 2
    wave = 2 * np.arange(half // 2)[None, None, :] + np.arange(2)[:, None, None]
    angle = 2.0 * math.pi / nx_len * (np.arange(half)[None, :, None] * wave % nx_len)
    return split_table(np.concatenate([np.cos(angle), -np.sin(angle)], axis=2))


def span_waves(nz_len):
    half = nz_len // 2
    wave = np.arange(half)
    return np.concatenate([wave, np.where(wave == 0, half, wave)])


def span_basis(points, nz_len):
    angle = 2.0 * math.pi / nz_len * (points[:, None] * span_waves(nz_len)[None, :] % nz_len)
    cosine = np.arange(nz_len)[None, :] <= nz_len // 2
    return np.where(cosine, np.cos(angle), np.sin(angle))


def plane_table(nz_len, groups):
    span = nz_len // groups
    block = np.arange(groups) * span
    return split_table(span_basis(np.concatenate([block - 1, block + span]) % nz_len, nz_len))


def cell_table(nz_len, groups):
    return split_table(span_basis(np.arange(nz_len).reshape(groups, -1).T.reshape(-1), nz_len))


def sine_matrix(span):
    index = np.arange(1, span + 1)
    return np.sin(math.pi / (span + 1) * index[:, None] * index[None, :])


def halves(values):
    high = values.astype(jnp.bfloat16)
    low = (values - high.astype(jnp.float32)).astype(jnp.bfloat16)
    return high, low


def dot3(a, b, dims):
    def one(left, right):
        return lax.dot_general(left, right, (dims, ((), ())), preferred_element_type=jnp.float32)

    return one(a[0], b[0]) + (one(a[0], b[1]) + one(a[1], b[0]))


def swap_bits(tiles):
    tiles = list(tiles)
    lanes = tiles[0].shape[1]
    lane = lax.broadcasted_iota(jnp.int32, tiles[0].shape, 1)
    bit = len(tiles) // 2
    while bit:
        upper = (lane & bit) != 0
        for first in range(len(tiles)):
            if first & bit:
                continue
            a, b = tiles[first], tiles[first | bit]
            tiles[first] = jnp.where(upper, pltpu.roll(b, bit, 1), a)
            tiles[first | bit] = jnp.where(upper, b, pltpu.roll(a, lanes - bit, 1))
        bit //= 2
    return tiles


def turn(value, shift):
    lanes = value.shape[1]
    return value if shift % lanes == 0 else pltpu.roll(value, shift % lanes, 1)


def both(values):
    return jnp.concatenate([values, values], axis=0)


def wide(values):
    half = values.shape[1] // 2
    low, high = values[:, :half], values[:, half:]
    return jnp.concatenate([low, low, high, high], axis=1)


def local_forward(place_ref, lower_in, upper_in, sigma_ref, weight_ref, rhs_ref, stream_ref, sine_ref, rows_ref, inv_ref, send_ref, sol_ref, ratio_ref, value_ref, state_ref, edges_ref, lower_ref, upper_ref, sems):
    some, span, nx_len = rows_ref.shape
    rows = sol_ref.shape[0]
    half = nx_len // 2
    index = pl.program_id(0)
    steps = rows // some

    @pl.when(index == 0)
    def _():
        pltpu.make_async_copy(lower_in, lower_ref, sems.at[0]).start()
        pltpu.make_async_copy(upper_in, upper_ref, sems.at[1]).start()
        value_ref[...] = jnp.zeros_like(value_ref)
        state_ref[...] = jnp.ones_like(state_ref)

    field = rhs_ref[...].reshape(some * span, nx_len)
    first, second = field[:, :half], field[:, half:]
    parts = []
    for parity, folded in enumerate((first + second, first - second)):
        parts.append(dot3(halves(folded), (stream_ref[0, parity], stream_ref[1, parity]), ((1,), (0,))))
    lane = lax.broadcasted_iota(jnp.int32, (1, nx_len), 1)
    scale = jnp.where(lane == 0, 1.0 / nx_len, 2.0 / nx_len)
    modes = jnp.concatenate(parts, axis=1) * scale
    modes = dot3((sine_ref[0], sine_ref[1]), halves(modes), ((1,), (0,)))
    rows_ref[...] = modes.reshape(some, span, nx_len)

    @pl.when(index == 0)
    def _():
        pltpu.make_async_copy(lower_in, lower_ref, sems.at[0]).wait()
        pltpu.make_async_copy(upper_in, upper_ref, sems.at[1]).wait()

    base = place_ref[1] * rows
    sigma = sigma_ref[...]
    step = 8

    def descend(chunk, carry):
        value, numer, denom = carry
        for k in range(step):
            row = chunk * step + k
            cell = index * some + row
            low, high = lower_ref[base + cell], upper_ref[base + cell]
            numer = low * numer + sigma * denom
            new = numer + high * denom
            inv = denom / new
            denom = new
            inv_ref[row] = inv
            ratio_ref[cell] = high * inv
            value = (low * value - rows_ref[row]) * wide(inv)
            sol_ref[cell] = value
        return value, numer, denom

    value, numer, denom = lax.fori_loop(
        0, some // step, descend, (value_ref[...], state_ref[0], state_ref[1])
    )
    value_ref[...] = value
    state_ref[0] = numer
    state_ref[1] = denom

    @pl.when(index == steps - 1)
    def _():
        weight = weight_ref[0] * (2.0 / ((span + 1) * span_weight))

        def ascend(chunk, value):
            for k in range(step):
                row = rows - 1 - (chunk * step + k)
                value = sol_ref[row] + wide(ratio_ref[row]) * value
                sol_ref[row] = value
                part = weight * value
                part = part[: span // 2] + part[span // 2 :]
                part = part + pltpu.roll(part, 4, 0)
                part = part + pltpu.roll(part, 2, 0)
                other = pltpu.roll(part, 1, 0)
                edges_ref[pl.ds(row, 1)] = (part + other)[:1]
                edges_ref[pl.ds(rows + row, 1)] = (part - other)[:1]
            return value

        lax.fori_loop(0, rows // step, ascend, jnp.zeros((span, nx_len), jnp.float32))
        sines = (sine_ref[0, :span, :span], sine_ref[1, :span, :span])
        for side, row in enumerate((0, rows - 1)):
            edge = dot3(sines, halves(sol_ref[row]), ((1,), (0,))) * (2.0 / (span + 1))
            edges_ref[2 * rows + side * span : 2 * rows + side * span + span] = edge
        groups, both_parts, _ = send_ref.shape
        count = both_parts // 2
        quarter = nx_len // 4
        for tile in range(4):
            turned = edges_ref[:, tile * quarter : tile * quarter + quarter].T
            place = tile // 2 * (groups // 2)
            part = tile % 2 * count
            send_ref[place : place + groups // 2, part : part + count] = turned.reshape(groups // 2, count, -1)


def local_inverse(place_ref, lower_ref, upper_ref, piece_ref, rows_ref, inv_ref, weight_ref, stream_ref, sine_ref, out_ref, sol_ref, edges_ref, value_ref):
    rows, span, nx_len = rows_ref.shape
    some = out_ref.shape[0]
    half = nx_len // 2
    index = pl.program_id(0)
    steps = rows // some
    base = place_ref[1] * rows

    def ascend(chunk, value):
        for row in reversed(range(chunk * some, chunk * some + some)):
            value = sol_ref[row] + wide(upper_ref[base + row] * inv_ref[row]) * value
            sol_ref[row] = value
        value_ref[...] = value

    @pl.when(index == 0)
    def _():
        groups, both_parts, _ = piece_ref.shape
        count = both_parts // 2
        quarter = nx_len // 4
        for tile in range(4):
            place = tile // 2 * (groups // 2)
            part = tile % 2 * count
            block = piece_ref[place : place + groups // 2, part : part + count]
            edges_ref[:, tile * quarter : tile * quarter + quarter] = block.reshape(quarter, -1).T
        sines = (sine_ref[0, :span, :span], sine_ref[1, :span, :span])
        before = dot3(sines, halves(edges_ref[2 * rows : 2 * rows + span]), ((1,), (0,)))
        after = dot3(sines, halves(edges_ref[2 * rows + span :]), ((1,), (0,)))
        weight_low, weight_high = weight_ref[0], weight_ref[1]
        step = 8

        def descend(chunk, value):
            for k in range(step):
                row = chunk * step + k
                source = rows_ref[row] - weight_low * edges_ref[pl.ds(row, 1)] - weight_high * edges_ref[pl.ds(rows + row, 1)]
                value = (lower_ref[base + row] * value - source) * wide(inv_ref[row])
                sol_ref[row] = value
            return value

        lax.fori_loop(0, rows // step, descend, before)

        ascend(steps - 1, after)

    def transform(chunk):
        modes = sol_ref[chunk * some : chunk * some + some].reshape(some * span, nx_len)
        field = dot3((sine_ref[0], sine_ref[1]), halves(modes), ((1,), (0,))) * (2.0 / (span + 1))
        outs = []
        for parity in range(2):
            part = field[:, parity * half : parity * half + half]
            outs.append(dot3(halves(part), (stream_ref[0, parity], stream_ref[1, parity]), ((1,), (1,))))
        even, odd = outs
        out_ref[:, :, :half] = (even + odd).reshape(some, span, half)
        out_ref[:, :, half:] = (even - odd).reshape(some, span, half)

    for chunk in reversed(range(steps)):

        @pl.when(index == steps - 1 - chunk)
        def _(chunk=chunk):
            if chunk > 0:
                ascend(chunk - 1, value_ref[...])
            transform(chunk)


def factor(place_ref, lower_ref, upper_ref, waves_ref, both_ref, carry_down_ref, carry_up_ref, close_ref, start_ref):
    rows = both_ref.shape[1]
    blocks = carry_down_ref.shape[0]
    total = rows * blocks
    sigma = waves_ref[...]
    one = jnp.ones_like(sigma)
    step = 8

    def step_down(row, numer, denom):
        numer = lower_ref[row] * numer + sigma * denom
        return numer, numer + upper_ref[row] * denom

    def step_up(row, numer, denom):
        numer = upper_ref[row] * numer + sigma * denom
        return numer, numer + lower_ref[row] * denom

    def block(index, carry):
        t_down, t_up = carry
        other = blocks - 1 - index
        start_ref[0, index] = t_down
        start_ref[1, other] = t_up

        def some(chunk, inner):
            nd, dd, nu, du, prod_l, prod_u = inner
            for k in range(step):
                row = index * rows + chunk * step + k
                back = total - 1 - row
                nd, dd = step_down(row, nd, dd)
                nu, du = step_up(back, nu, du)
                prod_l = prod_l * lower_ref[row]
                prod_u = prod_u * upper_ref[back]
            return nd, dd, nu, du, prod_l, prod_u

        unit = jnp.float32(1.0)
        nd, dd, nu, du, prod_l, prod_u = lax.fori_loop(
            0, rows // step, some, (t_down, one, t_up, one, unit, unit)
        )
        inv_d = 1.0 / dd
        inv_u = 1.0 / du
        carry_down_ref[index] = prod_l * inv_d
        carry_up_ref[other] = prod_u * inv_u
        return nd * inv_d, nu * inv_u

    lax.fori_loop(0, blocks, block, (one, one))
    place = place_ref[1]
    first = place * rows

    def own(chunk, inner):
        nd, dd, nu, du = inner
        for k in range(step):
            row = chunk * step + k
            back = rows - 1 - row
            nd, new_d = step_down(first + row, nd, dd)
            both_ref[0, row] = dd / new_d
            nu, new_u = step_up(first + back, nu, du)
            both_ref[1, back] = du / new_u
            dd, du = new_d, new_u
        return nd, dd, nu, du

    nd, dd, nu, du = lax.fori_loop(
        0, rows // step, own, (start_ref[0, place], one, start_ref[1, place], one)
    )
    t_end = nd / dd
    t_next = start_ref[1, place]
    is_last = place == blocks - 1
    inner = jnp.where(is_last, 0.0, 1.0 / (t_next + t_end * (1.0 - t_next)))
    close_ref[0] = inner
    close_ref[1] = inner * (1.0 - t_next)
    close_ref[2] = 1.0 - start_ref[0, place]
    close_ref[3] = 1.0 - t_next


def span_forward(place_ref, lower_ref, upper_ref, piece_ref, factor_ref, close_ref, plane_ref, cell_ref, rows_ref, send_ref, edge_ref, keep_ref):
    groups, parts, lanes = piece_ref.shape
    rows, _, nz_len = rows_ref.shape
    span = nz_len // groups
    per = lanes // groups
    tiles = swap_bits([piece_ref[t] for t in range(groups)])
    lane = lax.broadcasted_iota(jnp.int32, (parts, lanes), 1)

    def source(value, group):
        return turn(tiles[value % groups], groups * (group - value // groups))

    for row in range(rows):
        pair = jnp.where(lane < groups, source(row, 0), source(rows + row, 1))
        keep_ref[row] = jnp.where(lane < 2 * groups, pair, 0.0)
    wave = lax.broadcasted_iota(jnp.int32, (1, nz_len), 1)
    scale = jnp.where(wave % (nz_len // 2) == 0, 1.0 / nz_len, 2.0 / nz_len)
    planes = keep_ref[...].reshape(rows * parts, lanes)
    spec = dot3(halves(planes), (plane_ref[0], plane_ref[1]), ((1,), (0,)))
    rows_ref[...] = (spec * (-span_weight * scale)).reshape(rows, parts, nz_len)
    cells = []
    for side in range(2):
        built = []
        for tile in range(nz_len // lanes):
            value = source(2 * rows + side * span + tile * per, 0)
            for group in range(1, per):
                other = source(2 * rows + side * span + tile * per + group, group)
                value = jnp.where(lane < groups * group, value, other)
            built.append(value)
        cells.append(jnp.concatenate(built, axis=1))
    edges = dot3(halves(jnp.concatenate(cells, axis=0)), (cell_ref[0], cell_ref[1]), ((1,), (0,))) * scale
    low_edge, high_edge = edges[:parts], edges[parts:]
    edge_ref[0] = low_edge
    edge_ref[1] = high_edge
    base = place_ref[1] * rows
    step = 8

    def sweep(chunk, carry):
        down, up = carry
        for k in range(step):
            row = chunk * step + k
            back = rows - 1 - row
            down = (lower_ref[base + row] * down - rows_ref[row]) * both(factor_ref[0, row])
            up = (upper_ref[base + back] * up - rows_ref[back]) * both(factor_ref[1, back])
        return down, up

    start = (both(close_ref[2]) * low_edge, both(close_ref[3]) * high_edge)
    down, up = lax.fori_loop(0, rows // step, sweep, start)
    send_ref[0] = down + high_edge
    send_ref[1] = up + low_edge


def span_inverse(place_ref, lower_ref, upper_ref, rows_ref, mate_ref, piece_ref, edge_ref, factor_ref, carry_down_ref, carry_up_ref, close_ref, plane_ref, cell_ref, *rest):
    *end_refs, out_ref, grow_ref, near_ref, ends_ref = rest
    groups, parts, lanes = out_ref.shape
    rows, _, nz_len = rows_ref.shape
    blocks = ends_ref.shape[0]
    span = nz_len // groups
    per = lanes // groups
    place = place_ref[1]
    base = place * rows
    step = 8
    zero = jnp.zeros((parts, nz_len), jnp.float32)
    pair = place // 2
    for shift, end_ref in enumerate(end_refs, 1):
        ends_ref[(pair + blocks - shift) % blocks] = end_ref[...]

    def rise(k, value):
        through = carry_down_ref[2 * k + 1] * carry_down_ref[2 * k]
        return ends_ref[k] + both(through) * value

    def climb(k, value):
        other = blocks - 1 - k
        through = carry_up_ref[2 * other + 1] * carry_up_ref[2 * other]
        return ends_ref[other] + both(through) * value

    before = lax.fori_loop(0, pair, rise, zero)
    after = lax.fori_loop(0, blocks - 1 - pair, climb, zero)
    odd = place % 2 == 1
    mate = jnp.where(odd, place - 1, place + 1)
    before = jnp.where(odd, mate_ref[0] + both(carry_down_ref[mate]) * before, before)
    after = jnp.where(odd, after, mate_ref[1] + both(carry_up_ref[mate]) * after)
    before = before + both(close_ref[2]) * edge_ref[0]
    after = after + both(close_ref[3]) * edge_ref[1]

    def descend(chunk, value):
        for k in range(step):
            row = chunk * step + k
            value = (lower_ref[base + row] * value - rows_ref[row]) * both(factor_ref[0, row])
            grow_ref[row] = value
        return value

    last = lax.fori_loop(0, rows // step, descend, before)
    beyond = both(close_ref[0]) * after + both(close_ref[1]) * last

    def ascend(chunk, value):
        for k in range(step):
            row = rows - 1 - (chunk * step + k)
            ratio = upper_ref[base + row] * factor_ref[0, row]
            value = grow_ref[row] + both(ratio) * value
            grow_ref[row] = value
        return value

    first = lax.fori_loop(0, rows // step, ascend, beyond)
    below = before + both(close_ref[2]) * first
    flat = grow_ref[...].reshape(rows * parts, nz_len)
    near = dot3(halves(flat), (plane_ref[0], plane_ref[1]), ((1,), (1,)))
    near_ref[...] = near.reshape(rows, parts, lanes)
    edges = jnp.concatenate([below, beyond], axis=0)
    cells = dot3(halves(edges), (cell_ref[0], cell_ref[1]), ((1,), (1,)))
    lane = lax.broadcasted_iota(jnp.int32, (parts, lanes), 1)
    def piece(value, group):
        if value < rows:
            return turn(near_ref[value], groups * group)
        if value < 2 * rows:
            return turn(near_ref[value - rows], groups * (group - 1))
        side, cell = divmod(value - 2 * rows, span)
        tile, part = divmod(cell, per)
        found = cells[side * parts : side * parts + parts, tile * lanes : tile * lanes + lanes]
        return turn(found, groups * (group - part))

    tiles = []
    for t in range(groups):
        value = piece(t, 0)
        for group in range(1, per):
            value = jnp.where(lane < groups * group, value, piece(groups * group + t, group))
        tiles.append(value)
    for t, value in enumerate(swap_bits(tiles)):
        left = turn(piece_ref[(t + groups - 1) % groups], -rows)
        right = turn(piece_ref[(t + 1) % groups], rows)
        own = jnp.where(lane < rows, left, jnp.where(lane < 2 * rows, right, 0.0))
        out_ref[t] = value + own


smem = pl.BlockSpec(memory_space=pltpu.SMEM)
vmem = pl.BlockSpec(memory_space=pltpu.VMEM)
far = pl.BlockSpec(memory_space=pl.ANY)


def local(rhs, lower, upper):
    rows, span, nx_len = rhs.shape
    groups = lax.axis_size("row")
    blocks = lax.axis_size("col")
    nz_len = span * groups
    modes = nx_len // 2 // groups
    parts = 2 * modes
    steps = 3
    some = rows // steps
    lanes = 2 * (rows + span)
    place = jnp.stack([lax.axis_index("row"), lax.axis_index("col")]).astype(jnp.int32)
    f32 = jnp.float32
    params = pltpu.CompilerParams(vmem_limit_bytes=40 * 1024 * 1024)
    stream = stream_table(nx_len)
    sines = split_table(np.kron(np.eye(some), sine_matrix(span)))
    plane = plane_table(nz_len, groups)
    plane = jnp.pad(plane, ((0, 0), (0, lanes - 2 * groups), (0, 0)))
    cell = cell_table(nz_len, groups)
    ends_of_block = sine_matrix(span)[[0, -1]] * span_weight
    weights = jnp.asarray(np.broadcast_to(ends_of_block[:, :, None], (2, span, nx_len)).astype(np.float32))

    def on_chip(*shape):
        return pltpu.VMEM(shape, f32)

    def on_hbm(value):
        return pltpu.with_memory_space_constraint(value, pltpu.HBM)

    def fixed(value):
        shape = value.shape
        return pl.BlockSpec(shape, lambda i: (0,) * len(shape))

    def exchange(value, axis):
        return lax.all_to_all(value, axis, split_axis=0, concat_axis=0, tiled=True)

    def stream_part(index):
        angle = 2.0 * math.pi / nx_len * index.astype(f32)
        return stream_weight * (2.0 - 2.0 * jnp.cos(angle))

    def span_part(index, count):
        angle = 2.0 * math.pi / count * index.astype(f32)
        return span_weight * (2.0 - 2.0 * jnp.cos(angle))

    quarter = nx_len // 4
    every = jnp.arange(nx_len // 2)
    kx = 2 * (every % quarter) + every // quarter
    kz = span_part(jnp.arange(1, span + 1), 2 * (span + 1))
    sigma_own = kz[:, None] + stream_part(kx)[None, :] + shift_value
    field_spec = pl.BlockSpec((some, span, nx_len), lambda i: (i, 0, 0))
    mode_spec = pl.BlockSpec((some, span, nx_len), lambda i: (i, 0, 0))
    inv_spec = pl.BlockSpec((some, span, nx_len // 2), lambda i: (i, 0, 0))
    own_rows, own_inv, send = pl.pallas_call(
        local_forward,
        grid=(steps,),
        in_specs=[smem, far, far, vmem, fixed(weights), field_spec, fixed(stream), fixed(sines)],
        out_specs=[mode_spec, inv_spec, vmem],
        out_shape=[
            pltpu.HBM((rows, span, nx_len), f32),
            pltpu.HBM((rows, span, nx_len // 2), f32),
            on_chip(groups, parts, lanes),
        ],
        scratch_shapes=[
            on_chip(rows, span, nx_len),
            on_chip(rows, span, nx_len // 2),
            on_chip(span, nx_len),
            on_chip(2, span, nx_len // 2),
            on_chip(lanes, nx_len),
            pltpu.SMEM(lower.shape, f32),
            pltpu.SMEM(upper.shape, f32),
            pltpu.SemaphoreType.DMA((2,)),
        ],
        compiler_params=params,
        name="local_forward",
    )(place, on_hbm(lower), on_hbm(upper), sigma_own, on_hbm(weights), on_hbm(rhs), on_hbm(stream), on_hbm(sines))
    piece = exchange(send, "row")

    order = place[0] * modes + jnp.arange(modes)
    kx = 2 * (order % quarter) + order // quarter
    kz = jnp.asarray(span_waves(nz_len).astype(np.int32))
    sigma = stream_part(kx)[:, None] + span_part(kz, nz_len)[None, :] + shift_value
    factors, carry_down, carry_up, close = pl.pallas_call(
        factor,
        in_specs=[smem, smem, smem, vmem],
        out_specs=[vmem] * 4,
        out_shape=[
            on_chip(2, rows, modes, nz_len),
            on_chip(blocks, modes, nz_len),
            on_chip(blocks, modes, nz_len),
            on_chip(4, modes, nz_len),
        ],
        scratch_shapes=[on_chip(2, blocks, modes, nz_len)],
        compiler_params=params,
        name="factor",
    )(place, lower, upper, sigma)

    mode_rows, ends, edges = pl.pallas_call(
        span_forward,
        in_specs=[smem, smem, smem] + [vmem] * 5,
        out_specs=[vmem] * 3,
        out_shape=[
            on_chip(rows, parts, nz_len),
            on_chip(2, parts, nz_len),
            on_chip(2, parts, nz_len),
        ],
        scratch_shapes=[on_chip(rows, parts, lanes)],
        compiler_params=params,
        name="span_forward",
    )(place, lower, upper, piece, factors, close, plane, cell)
    mate = lax.ppermute(ends, "col", [(k, k ^ 1) for k in range(blocks)])
    odd = place[1] % 2 == 1
    pair = place[1] // 2

    def twice(value):
        return jnp.concatenate([value, value], axis=0)

    lower_ends, upper_ends = jnp.where(odd, mate, ends), jnp.where(odd, ends, mate)
    through_down = lax.dynamic_index_in_dim(carry_down, 2 * pair + 1, 0, keepdims=False)
    through_up = lax.dynamic_index_in_dim(carry_up, 2 * pair, 0, keepdims=False)
    down = upper_ends[0] + twice(through_down) * lower_ends[0]
    up = lower_ends[1] + twice(through_up) * upper_ends[1]
    chips = blocks // 2
    ends = []
    for shift in range(1, chips):
        message = jnp.where(pair + shift < chips, down, up)
        route = [(k, (k + 2 * shift) % blocks) for k in range(blocks)]
        ends.append(lax.ppermute(message, "col", route))

    send = pl.pallas_call(
        span_inverse,
        in_specs=[smem, smem, smem] + [vmem] * (10 + len(ends)),
        out_specs=vmem,
        out_shape=on_chip(groups, parts, lanes),
        scratch_shapes=[
            on_chip(rows, parts, nz_len),
            on_chip(rows, parts, lanes),
            on_chip(chips, parts, nz_len),
        ],
        compiler_params=params,
        name="span_inverse",
    )(place, lower, upper, mode_rows, mate, piece, edges, factors, carry_down, carry_up, close, plane, cell, *ends)
    piece = exchange(send, "row")

    return pl.pallas_call(
        local_inverse,
        grid=(steps,),
        in_specs=[smem, smem, smem] + [vmem] * 6,
        out_specs=pl.BlockSpec((some, span, nx_len), lambda i: (steps - 1 - i, 0, 0)),
        out_shape=jax.ShapeDtypeStruct((rows, span, nx_len), f32),
        scratch_shapes=[on_chip(rows, span, nx_len), on_chip(lanes, nx_len), on_chip(span, nx_len)],
        compiler_params=params,
        name="local_inverse",
    )(place, lower, upper, piece, own_rows, own_inv, weights, stream, sines)


def solution(mesh):
    return jax.shard_map(
        local,
        mesh=mesh,
        in_specs=(P("col", "row", None), P(), P()),
        out_specs=P("col", "row", None),
        check_vma=False,
    )
```

```python
import math

import jax
import jax.numpy as jnp
import ml_dtypes
import numpy as np
from jax import lax
from jax.experimental import pallas as pl
from jax.experimental.pallas import tpu as pltpu
from jax.sharding import PartitionSpec as P

stream_weight = 0.04
span_weight = 0.16
shift_value = 0.0002


def split_table(values):
    high = values.astype(ml_dtypes.bfloat16)
    low = (values - high.astype(np.float64)).astype(ml_dtypes.bfloat16)
    return jnp.asarray(np.stack([high, low]))


def stream_table(nx_len):
    half = nx_len // 2
    wave = 2 * np.arange(half // 2)[None, None, :] + np.arange(2)[:, None, None]
    angle = 2.0 * math.pi / nx_len * (np.arange(half)[None, :, None] * wave % nx_len)
    return split_table(np.concatenate([np.cos(angle), -np.sin(angle)], axis=2))


def span_waves(nz_len):
    half = nz_len // 2
    wave = np.arange(half)
    return np.concatenate([wave, np.where(wave == 0, half, wave)])


def span_basis(points, nz_len):
    angle = 2.0 * math.pi / nz_len * (points[:, None] * span_waves(nz_len)[None, :] % nz_len)
    cosine = np.arange(nz_len)[None, :] <= nz_len // 2
    return np.where(cosine, np.cos(angle), np.sin(angle))


def plane_table(nz_len, groups):
    span = nz_len // groups
    block = np.arange(groups) * span
    return split_table(span_basis(np.concatenate([block - 1, block + span]) % nz_len, nz_len))


def cell_table(nz_len, groups):
    return split_table(span_basis(np.arange(nz_len).reshape(groups, -1).T.reshape(-1), nz_len))


def sine_matrix(span):
    index = np.arange(1, span + 1)
    return np.sin(math.pi / (span + 1) * index[:, None] * index[None, :])


def halves(values):
    high = values.astype(jnp.bfloat16)
    low = (values - high.astype(jnp.float32)).astype(jnp.bfloat16)
    return high, low


def dot3(a, b, dims):
    def one(left, right):
        return lax.dot_general(left, right, (dims, ((), ())), preferred_element_type=jnp.float32)

    count = a[0].shape[0]
    tall = one(jnp.concatenate([a[0], a[1]], axis=0), b[0])
    return tall[:count] + (one(a[0], b[1]) + tall[count:])


def swap_bits(tiles):
    tiles = list(tiles)
    lanes = tiles[0].shape[1]
    lane = lax.broadcasted_iota(jnp.int32, tiles[0].shape, 1)
    bit = len(tiles) // 2
    while bit:
        upper = (lane & bit) != 0
        for first in range(len(tiles)):
            if first & bit:
                continue
            a, b = tiles[first], tiles[first | bit]
            tiles[first] = jnp.where(upper, pltpu.roll(b, bit, 1), a)
            tiles[first | bit] = jnp.where(upper, b, pltpu.roll(a, lanes - bit, 1))
        bit //= 2
    return tiles


def turn(value, shift):
    lanes = value.shape[1]
    return value if shift % lanes == 0 else pltpu.roll(value, shift % lanes, 1)


def both(values):
    return jnp.concatenate([values, values], axis=0)


def wide(values):
    half = values.shape[1] // 2
    low, high = values[:, :half], values[:, half:]
    return jnp.concatenate([low, low, high, high], axis=1)


def local_forward(place_ref, lower_in, upper_in, sigma_ref, weight_ref, rhs_ref, stream_ref, sine_ref, rows_ref, inv_ref, send_ref, sol_ref, ratio_ref, value_ref, state_ref, edges_ref, lower_ref, upper_ref, sems):
    some, span, nx_len = rows_ref.shape
    rows = sol_ref.shape[0]
    half = nx_len // 2
    index = pl.program_id(0)
    steps = rows // some

    @pl.when(index == 0)
    def _():
        pltpu.make_async_copy(lower_in, lower_ref, sems.at[0]).start()
        pltpu.make_async_copy(upper_in, upper_ref, sems.at[1]).start()
        value_ref[...] = jnp.zeros_like(value_ref)
        state_ref[...] = jnp.ones_like(state_ref)

    field = rhs_ref[...].reshape(some * span, nx_len)
    first, second = field[:, :half], field[:, half:]
    parts = []
    for parity, folded in enumerate((first + second, first - second)):
        parts.append(dot3(halves(folded), (stream_ref[0, parity], stream_ref[1, parity]), ((1,), (0,))))
    lane = lax.broadcasted_iota(jnp.int32, (1, nx_len), 1)
    scale = jnp.where(lane == 0, 1.0 / nx_len, 2.0 / nx_len)
    modes = jnp.concatenate(parts, axis=1) * scale
    modes = dot3((sine_ref[0], sine_ref[1]), halves(modes), ((1,), (0,)))
    rows_ref[...] = modes.reshape(some, span, nx_len)

    @pl.when(index == 0)
    def _():
        pltpu.make_async_copy(lower_in, lower_ref, sems.at[0]).wait()
        pltpu.make_async_copy(upper_in, upper_ref, sems.at[1]).wait()

    base = place_ref[1] * rows
    sigma = sigma_ref[...]
    step = 8

    def descend(chunk, carry):
        value, numer, denom = carry
        for k in range(step):
            row = chunk * step + k
            cell = index * some + row
            low, high = lower_ref[base + cell], upper_ref[base + cell]
            numer = low * numer + sigma * denom
            new = numer + high * denom
            inv = denom / new
            denom = new
            inv_ref[row] = inv
            ratio_ref[cell] = high * inv
            value = (low * value - rows_ref[row]) * wide(inv)
            sol_ref[cell] = value
        return value, numer, denom

    value, numer, denom = lax.fori_loop(
        0, some // step, descend, (value_ref[...], state_ref[0], state_ref[1])
    )
    value_ref[...] = value
    state_ref[0] = numer
    state_ref[1] = denom

    @pl.when(index == steps - 1)
    def _():
        weight = weight_ref[0] * (2.0 / ((span + 1) * span_weight))

        def ascend(chunk, value):
            for k in range(step):
                row = rows - 1 - (chunk * step + k)
                value = sol_ref[row] + wide(ratio_ref[row]) * value
                sol_ref[row] = value
                part = weight * value
                part = part[: span // 2] + part[span // 2 :]
                part = part + pltpu.roll(part, 4, 0)
                part = part + pltpu.roll(part, 2, 0)
                other = pltpu.roll(part, 1, 0)
                edges_ref[pl.ds(row, 1)] = (part + other)[:1]
                edges_ref[pl.ds(rows + row, 1)] = (part - other)[:1]
            return value

        lax.fori_loop(0, rows // step, ascend, jnp.zeros((span, nx_len), jnp.float32))
        sines = (sine_ref[0, :span, :span], sine_ref[1, :span, :span])
        for side, row in enumerate((0, rows - 1)):
            edge = dot3(sines, halves(sol_ref[row]), ((1,), (0,))) * (2.0 / (span + 1))
            edges_ref[2 * rows + side * span : 2 * rows + side * span + span] = edge
        groups, both_parts, _ = send_ref.shape
        count = both_parts // 2
        quarter = nx_len // 4
        for tile in range(4):
            turned = edges_ref[:, tile * quarter : tile * quarter + quarter].T
            place = tile // 2 * (groups // 2)
            part = tile % 2 * count
            send_ref[place : place + groups // 2, part : part + count] = turned.reshape(groups // 2, count, -1)


def local_inverse(place_ref, lower_ref, upper_ref, piece_ref, rows_ref, inv_ref, weight_ref, stream_ref, sine_ref, out_ref, sol_ref, edges_ref, value_ref):
    rows, span, nx_len = rows_ref.shape
    some = out_ref.shape[0]
    half = nx_len // 2
    index = pl.program_id(0)
    steps = rows // some
    base = place_ref[1] * rows

    def ascend(chunk, value):
        for row in reversed(range(chunk * some, chunk * some + some)):
            value = sol_ref[row] + wide(upper_ref[base + row] * inv_ref[row]) * value
            sol_ref[row] = value
        value_ref[...] = value

    @pl.when(index == 0)
    def _():
        groups, both_parts, _ = piece_ref.shape
        count = both_parts // 2
        quarter = nx_len // 4
        for tile in range(4):
            place = tile // 2 * (groups // 2)
            part = tile % 2 * count
            block = piece_ref[place : place + groups // 2, part : part + count]
            edges_ref[:, tile * quarter : tile * quarter + quarter] = block.reshape(quarter, -1).T
        sines = (sine_ref[0, :span, :span], sine_ref[1, :span, :span])
        before = dot3(sines, halves(edges_ref[2 * rows : 2 * rows + span]), ((1,), (0,)))
        after = dot3(sines, halves(edges_ref[2 * rows + span :]), ((1,), (0,)))
        weight_low, weight_high = weight_ref[0], weight_ref[1]
        step = 8

        def descend(chunk, value):
            for k in range(step):
                row = chunk * step + k
                source = rows_ref[row] - weight_low * edges_ref[pl.ds(row, 1)] - weight_high * edges_ref[pl.ds(rows + row, 1)]
                value = (lower_ref[base + row] * value - source) * wide(inv_ref[row])
                sol_ref[row] = value
            return value

        lax.fori_loop(0, rows // step, descend, before)

        ascend(steps - 1, after)

    def transform(chunk):
        modes = sol_ref[chunk * some : chunk * some + some].reshape(some * span, nx_len)
        field = dot3((sine_ref[0], sine_ref[1]), halves(modes), ((1,), (0,))) * (2.0 / (span + 1))
        outs = []
        for parity in range(2):
            part = field[:, parity * half : parity * half + half]
            outs.append(dot3(halves(part), (stream_ref[0, parity], stream_ref[1, parity]), ((1,), (1,))))
        even, odd = outs
        out_ref[:, :, :half] = (even + odd).reshape(some, span, half)
        out_ref[:, :, half:] = (even - odd).reshape(some, span, half)

    for chunk in reversed(range(steps)):

        @pl.when(index == steps - 1 - chunk)
        def _(chunk=chunk):
            if chunk > 0:
                ascend(chunk - 1, value_ref[...])
            transform(chunk)


def factor(place_ref, lower_ref, upper_ref, waves_ref, both_ref, carry_down_ref, carry_up_ref, close_ref, start_ref):
    rows = both_ref.shape[1]
    blocks = carry_down_ref.shape[0]
    total = rows * blocks
    sigma = waves_ref[...]
    one = jnp.ones_like(sigma)
    step = 8

    def step_down(row, numer, denom):
        numer = lower_ref[row] * numer + sigma * denom
        return numer, numer + upper_ref[row] * denom

    def step_up(row, numer, denom):
        numer = upper_ref[row] * numer + sigma * denom
        return numer, numer + lower_ref[row] * denom

    def block(index, carry):
        t_down, t_up = carry
        other = blocks - 1 - index
        start_ref[0, index] = t_down
        start_ref[1, other] = t_up

        def some(chunk, inner):
            nd, dd, nu, du, prod_l, prod_u = inner
            for k in range(step):
                row = index * rows + chunk * step + k
                back = total - 1 - row
                nd, dd = step_down(row, nd, dd)
                nu, du = step_up(back, nu, du)
                prod_l = prod_l * lower_ref[row]
                prod_u = prod_u * upper_ref[back]
            return nd, dd, nu, du, prod_l, prod_u

        unit = jnp.float32(1.0)
        nd, dd, nu, du, prod_l, prod_u = lax.fori_loop(
            0, rows // step, some, (t_down, one, t_up, one, unit, unit)
        )
        inv_d = 1.0 / dd
        inv_u = 1.0 / du
        carry_down_ref[index] = prod_l * inv_d
        carry_up_ref[other] = prod_u * inv_u
        return nd * inv_d, nu * inv_u

    lax.fori_loop(0, blocks, block, (one, one))
    place = place_ref[1]
    first = place * rows

    def own(chunk, inner):
        nd, dd, nu, du = inner
        for k in range(step):
            row = chunk * step + k
            back = rows - 1 - row
            nd, new_d = step_down(first + row, nd, dd)
            both_ref[0, row] = dd / new_d
            nu, new_u = step_up(first + back, nu, du)
            both_ref[1, back] = du / new_u
            dd, du = new_d, new_u
        return nd, dd, nu, du

    nd, dd, nu, du = lax.fori_loop(
        0, rows // step, own, (start_ref[0, place], one, start_ref[1, place], one)
    )
    t_end = nd / dd
    t_next = start_ref[1, place]
    is_last = place == blocks - 1
    inner = jnp.where(is_last, 0.0, 1.0 / (t_next + t_end * (1.0 - t_next)))
    close_ref[0] = inner
    close_ref[1] = inner * (1.0 - t_next)
    close_ref[2] = 1.0 - start_ref[0, place]
    close_ref[3] = 1.0 - t_next


def span_forward(place_ref, lower_ref, upper_ref, piece_ref, factor_ref, close_ref, plane_ref, cell_ref, rows_ref, send_ref, edge_ref, keep_ref):
    groups, parts, lanes = piece_ref.shape
    rows, _, nz_len = rows_ref.shape
    span = nz_len // groups
    per = lanes // groups
    tiles = swap_bits([piece_ref[t] for t in range(groups)])
    lane = lax.broadcasted_iota(jnp.int32, (parts, lanes), 1)

    def source(value, group):
        return turn(tiles[value % groups], groups * (group - value // groups))

    for row in range(rows):
        pair = jnp.where(lane < groups, source(row, 0), source(rows + row, 1))
        keep_ref[row] = jnp.where(lane < 2 * groups, pair, 0.0)
    wave = lax.broadcasted_iota(jnp.int32, (1, nz_len), 1)
    scale = jnp.where(wave % (nz_len // 2) == 0, 1.0 / nz_len, 2.0 / nz_len)
    planes = keep_ref[...].reshape(rows * parts, lanes)
    spec = dot3(halves(planes), (plane_ref[0], plane_ref[1]), ((1,), (0,)))
    rows_ref[...] = (spec * (-span_weight * scale)).reshape(rows, parts, nz_len)
    cells = []
    for side in range(2):
        built = []
        for tile in range(nz_len // lanes):
            value = source(2 * rows + side * span + tile * per, 0)
            for group in range(1, per):
                other = source(2 * rows + side * span + tile * per + group, group)
                value = jnp.where(lane < groups * group, value, other)
            built.append(value)
        cells.append(jnp.concatenate(built, axis=1))
    edges = dot3(halves(jnp.concatenate(cells, axis=0)), (cell_ref[0], cell_ref[1]), ((1,), (0,))) * scale
    low_edge, high_edge = edges[:parts], edges[parts:]
    edge_ref[0] = low_edge
    edge_ref[1] = high_edge
    base = place_ref[1] * rows
    step = 8

    def sweep(chunk, carry):
        down, up = carry
        for k in range(step):
            row = chunk * step + k
            back = rows - 1 - row
            down = (lower_ref[base + row] * down - rows_ref[row]) * both(factor_ref[0, row])
            up = (upper_ref[base + back] * up - rows_ref[back]) * both(factor_ref[1, back])
        return down, up

    start = (both(close_ref[2]) * low_edge, both(close_ref[3]) * high_edge)
    down, up = lax.fori_loop(0, rows // step, sweep, start)
    send_ref[0] = down + high_edge
    send_ref[1] = up + low_edge


def span_inverse(place_ref, lower_ref, upper_ref, rows_ref, mate_ref, piece_ref, edge_ref, factor_ref, carry_down_ref, carry_up_ref, close_ref, plane_ref, cell_ref, *rest):
    *end_refs, out_ref, grow_ref, near_ref, ends_ref = rest
    groups, parts, lanes = out_ref.shape
    rows, _, nz_len = rows_ref.shape
    blocks = ends_ref.shape[0]
    span = nz_len // groups
    per = lanes // groups
    place = place_ref[1]
    base = place * rows
    step = 8
    zero = jnp.zeros((parts, nz_len), jnp.float32)
    pair = place // 2
    for shift, end_ref in enumerate(end_refs, 1):
        ends_ref[(pair + blocks - shift) % blocks] = end_ref[...]

    def rise(k, value):
        through = carry_down_ref[2 * k + 1] * carry_down_ref[2 * k]
        return ends_ref[k] + both(through) * value

    def climb(k, value):
        other = blocks - 1 - k
        through = carry_up_ref[2 * other + 1] * carry_up_ref[2 * other]
        return ends_ref[other] + both(through) * value

    before = lax.fori_loop(0, pair, rise, zero)
    after = lax.fori_loop(0, blocks - 1 - pair, climb, zero)
    odd = place % 2 == 1
    mate = jnp.where(odd, place - 1, place + 1)
    before = jnp.where(odd, mate_ref[0] + both(carry_down_ref[mate]) * before, before)
    after = jnp.where(odd, after, mate_ref[1] + both(carry_up_ref[mate]) * after)
    before = before + both(close_ref[2]) * edge_ref[0]
    after = after + both(close_ref[3]) * edge_ref[1]

    def descend(chunk, value):
        for k in range(step):
            row = chunk * step + k
            value = (lower_ref[base + row] * value - rows_ref[row]) * both(factor_ref[0, row])
            grow_ref[row] = value
        return value

    last = lax.fori_loop(0, rows // step, descend, before)
    beyond = both(close_ref[0]) * after + both(close_ref[1]) * last

    def ascend(chunk, value):
        for k in range(step):
            row = rows - 1 - (chunk * step + k)
            ratio = upper_ref[base + row] * factor_ref[0, row]
            value = grow_ref[row] + both(ratio) * value
            grow_ref[row] = value
        return value

    first = lax.fori_loop(0, rows // step, ascend, beyond)
    below = before + both(close_ref[2]) * first
    flat = grow_ref[...].reshape(rows * parts, nz_len)
    near = dot3(halves(flat), (plane_ref[0], plane_ref[1]), ((1,), (1,)))
    near_ref[...] = near.reshape(rows, parts, lanes)
    edges = jnp.concatenate([below, beyond], axis=0)
    cells = dot3(halves(edges), (cell_ref[0], cell_ref[1]), ((1,), (1,)))
    lane = lax.broadcasted_iota(jnp.int32, (parts, lanes), 1)
    def piece(value, group):
        if value < rows:
            return turn(near_ref[value], groups * group)
        if value < 2 * rows:
            return turn(near_ref[value - rows], groups * (group - 1))
        side, cell = divmod(value - 2 * rows, span)
        tile, part = divmod(cell, per)
        found = cells[side * parts : side * parts + parts, tile * lanes : tile * lanes + lanes]
        return turn(found, groups * (group - part))

    tiles = []
    for t in range(groups):
        value = piece(t, 0)
        for group in range(1, per):
            value = jnp.where(lane < groups * group, value, piece(groups * group + t, group))
        tiles.append(value)
    for t, value in enumerate(swap_bits(tiles)):
        left = turn(piece_ref[(t + groups - 1) % groups], -rows)
        right = turn(piece_ref[(t + 1) % groups], rows)
        own = jnp.where(lane < rows, left, jnp.where(lane < 2 * rows, right, 0.0))
        out_ref[t] = value + own


smem = pl.BlockSpec(memory_space=pltpu.SMEM)
vmem = pl.BlockSpec(memory_space=pltpu.VMEM)
far = pl.BlockSpec(memory_space=pl.ANY)


def local(rhs, lower, upper):
    rows, span, nx_len = rhs.shape
    groups = lax.axis_size("row")
    blocks = lax.axis_size("col")
    nz_len = span * groups
    modes = nx_len // 2 // groups
    parts = 2 * modes
    steps = 3
    some = rows // steps
    lanes = 2 * (rows + span)
    place = jnp.stack([lax.axis_index("row"), lax.axis_index("col")]).astype(jnp.int32)
    f32 = jnp.float32
    params = pltpu.CompilerParams(vmem_limit_bytes=40 * 1024 * 1024)
    stream = stream_table(nx_len)
    sines = split_table(np.kron(np.eye(some), sine_matrix(span)))
    plane = plane_table(nz_len, groups)
    plane = jnp.pad(plane, ((0, 0), (0, lanes - 2 * groups), (0, 0)))
    cell = cell_table(nz_len, groups)
    ends_of_block = sine_matrix(span)[[0, -1]] * span_weight
    weights = jnp.asarray(np.broadcast_to(ends_of_block[:, :, None], (2, span, nx_len)).astype(np.float32))

    def on_chip(*shape):
        return pltpu.VMEM(shape, f32)

    def on_hbm(value):
        return pltpu.with_memory_space_constraint(value, pltpu.HBM)

    def fixed(value):
        shape = value.shape
        return pl.BlockSpec(shape, lambda i: (0,) * len(shape))

    def exchange(value, axis):
        return lax.all_to_all(value, axis, split_axis=0, concat_axis=0, tiled=True)

    def stream_part(index):
        angle = 2.0 * math.pi / nx_len * index.astype(f32)
        return stream_weight * (2.0 - 2.0 * jnp.cos(angle))

    def span_part(index, count):
        angle = 2.0 * math.pi / count * index.astype(f32)
        return span_weight * (2.0 - 2.0 * jnp.cos(angle))

    quarter = nx_len // 4
    every = jnp.arange(nx_len // 2)
    kx = 2 * (every % quarter) + every // quarter
    kz = span_part(jnp.arange(1, span + 1), 2 * (span + 1))
    sigma_own = kz[:, None] + stream_part(kx)[None, :] + shift_value
    field_spec = pl.BlockSpec((some, span, nx_len), lambda i: (i, 0, 0))
    mode_spec = pl.BlockSpec((some, span, nx_len), lambda i: (i, 0, 0))
    inv_spec = pl.BlockSpec((some, span, nx_len // 2), lambda i: (i, 0, 0))
    own_rows, own_inv, send = pl.pallas_call(
        local_forward,
        grid=(steps,),
        in_specs=[smem, far, far, vmem, fixed(weights), field_spec, fixed(stream), fixed(sines)],
        out_specs=[mode_spec, inv_spec, vmem],
        out_shape=[
            pltpu.HBM((rows, span, nx_len), f32),
            pltpu.HBM((rows, span, nx_len // 2), f32),
            on_chip(groups, parts, lanes),
        ],
        scratch_shapes=[
            on_chip(rows, span, nx_len),
            on_chip(rows, span, nx_len // 2),
            on_chip(span, nx_len),
            on_chip(2, span, nx_len // 2),
            on_chip(lanes, nx_len),
            pltpu.SMEM(lower.shape, f32),
            pltpu.SMEM(upper.shape, f32),
            pltpu.SemaphoreType.DMA((2,)),
        ],
        compiler_params=params,
        name="local_forward",
    )(place, on_hbm(lower), on_hbm(upper), sigma_own, on_hbm(weights), on_hbm(rhs), on_hbm(stream), on_hbm(sines))
    piece = exchange(send, "row")

    order = place[0] * modes + jnp.arange(modes)
    kx = 2 * (order % quarter) + order // quarter
    kz = jnp.asarray(span_waves(nz_len).astype(np.int32))
    sigma = stream_part(kx)[:, None] + span_part(kz, nz_len)[None, :] + shift_value
    factors, carry_down, carry_up, close = pl.pallas_call(
        factor,
        in_specs=[smem, smem, smem, vmem],
        out_specs=[vmem] * 4,
        out_shape=[
            on_chip(2, rows, modes, nz_len),
            on_chip(blocks, modes, nz_len),
            on_chip(blocks, modes, nz_len),
            on_chip(4, modes, nz_len),
        ],
        scratch_shapes=[on_chip(2, blocks, modes, nz_len)],
        compiler_params=params,
        name="factor",
    )(place, lower, upper, sigma)

    mode_rows, ends, edges = pl.pallas_call(
        span_forward,
        in_specs=[smem, smem, smem] + [vmem] * 5,
        out_specs=[vmem] * 3,
        out_shape=[
            on_chip(rows, parts, nz_len),
            on_chip(2, parts, nz_len),
            on_chip(2, parts, nz_len),
        ],
        scratch_shapes=[on_chip(rows, parts, lanes)],
        compiler_params=params,
        name="span_forward",
    )(place, lower, upper, piece, factors, close, plane, cell)
    mate = lax.ppermute(ends, "col", [(k, k ^ 1) for k in range(blocks)])
    odd = place[1] % 2 == 1
    pair = place[1] // 2

    def twice(value):
        return jnp.concatenate([value, value], axis=0)

    lower_ends, upper_ends = jnp.where(odd, mate, ends), jnp.where(odd, ends, mate)
    through_down = lax.dynamic_index_in_dim(carry_down, 2 * pair + 1, 0, keepdims=False)
    through_up = lax.dynamic_index_in_dim(carry_up, 2 * pair, 0, keepdims=False)
    down = upper_ends[0] + twice(through_down) * lower_ends[0]
    up = lower_ends[1] + twice(through_up) * upper_ends[1]
    chips = blocks // 2
    ends = []
    for shift in range(1, chips):
        message = jnp.where(pair + shift < chips, down, up)
        route = [(k, (k + 2 * shift) % blocks) for k in range(blocks)]
        ends.append(lax.ppermute(message, "col", route))

    send = pl.pallas_call(
        span_inverse,
        in_specs=[smem, smem, smem] + [vmem] * (10 + len(ends)),
        out_specs=vmem,
        out_shape=on_chip(groups, parts, lanes),
        scratch_shapes=[
            on_chip(rows, parts, nz_len),
            on_chip(rows, parts, lanes),
            on_chip(chips, parts, nz_len),
        ],
        compiler_params=params,
        name="span_inverse",
    )(place, lower, upper, mode_rows, mate, piece, edges, factors, carry_down, carry_up, close, plane, cell, *ends)
    piece = exchange(send, "row")

    return pl.pallas_call(
        local_inverse,
        grid=(steps,),
        in_specs=[smem, smem, smem] + [vmem] * 6,
        out_specs=pl.BlockSpec((some, span, nx_len), lambda i: (steps - 1 - i, 0, 0)),
        out_shape=jax.ShapeDtypeStruct((rows, span, nx_len), f32),
        scratch_shapes=[on_chip(rows, span, nx_len), on_chip(lanes, nx_len), on_chip(span, nx_len)],
        compiler_params=params,
        name="local_inverse",
    )(place, lower, upper, piece, own_rows, own_inv, weights, stream, sines)


def solution(mesh):
    return jax.shard_map(
        local,
        mesh=mesh,
        in_specs=(P("col", "row", None), P(), P()),
        out_specs=P("col", "row", None),
        check_vma=False,
    )
```

```python
import math

import jax
import jax.numpy as jnp
import ml_dtypes
import numpy as np
from jax import lax
from jax.experimental import pallas as pl
from jax.experimental.pallas import tpu as pltpu
from jax.sharding import PartitionSpec as P

stream_weight = 0.04
span_weight = 0.16
shift_value = 0.0002


def split_table(values):
    high = values.astype(ml_dtypes.bfloat16)
    low = (values - high.astype(np.float64)).astype(ml_dtypes.bfloat16)
    return jnp.asarray(np.stack([high, low]))


def stream_table(nx_len):
    half = nx_len // 2
    wave = 2 * np.arange(half // 2)[None, None, :] + np.arange(2)[:, None, None]
    angle = 2.0 * math.pi / nx_len * (np.arange(half)[None, :, None] * wave % nx_len)
    return split_table(np.concatenate([np.cos(angle), -np.sin(angle)], axis=2))


def span_waves(nz_len):
    half = nz_len // 2
    wave = np.arange(half)
    return np.concatenate([wave, np.where(wave == 0, half, wave)])


def span_basis(points, nz_len):
    angle = 2.0 * math.pi / nz_len * (points[:, None] * span_waves(nz_len)[None, :] % nz_len)
    cosine = np.arange(nz_len)[None, :] <= nz_len // 2
    return np.where(cosine, np.cos(angle), np.sin(angle))


def plane_table(nz_len, groups):
    span = nz_len // groups
    block = np.arange(groups) * span
    return split_table(span_basis(np.concatenate([block - 1, block + span]) % nz_len, nz_len))


def cell_table(nz_len, groups):
    return split_table(span_basis(np.arange(nz_len).reshape(groups, -1).T.reshape(-1), nz_len))


def sine_matrix(span):
    index = np.arange(1, span + 1)
    return np.sin(math.pi / (span + 1) * index[:, None] * index[None, :])


def halves(values):
    high = values.astype(jnp.bfloat16)
    low = (values - high.astype(jnp.float32)).astype(jnp.bfloat16)
    return high, low


def dot3(a, b, dims):
    def one(left, right):
        return lax.dot_general(left, right, (dims, ((), ())), preferred_element_type=jnp.float32)

    count = a[0].shape[0]
    tall = one(jnp.concatenate([a[0], a[1]], axis=0), b[0])
    return tall[:count] + (one(a[0], b[1]) + tall[count:])


def swap_bits(tiles):
    tiles = list(tiles)
    lanes = tiles[0].shape[1]
    lane = lax.broadcasted_iota(jnp.int32, tiles[0].shape, 1)
    bit = len(tiles) // 2
    while bit:
        upper = (lane & bit) != 0
        for first in range(len(tiles)):
            if first & bit:
                continue
            a, b = tiles[first], tiles[first | bit]
            tiles[first] = jnp.where(upper, pltpu.roll(b, bit, 1), a)
            tiles[first | bit] = jnp.where(upper, b, pltpu.roll(a, lanes - bit, 1))
        bit //= 2
    return tiles


def turn(value, shift):
    lanes = value.shape[1]
    return value if shift % lanes == 0 else pltpu.roll(value, shift % lanes, 1)


def both(values):
    return jnp.concatenate([values, values], axis=0)


def wide(values):
    half = values.shape[1] // 2
    low, high = values[:, :half], values[:, half:]
    return jnp.concatenate([low, low, high, high], axis=1)


def local_forward(place_ref, lower_in, upper_in, sigma_ref, weight_ref, rhs_ref, stream_ref, sine_ref, rows_ref, inv_ref, send_ref, sol_ref, ratio_ref, value_ref, state_ref, edges_ref, lower_ref, upper_ref, sems):
    some, span, nx_len = rows_ref.shape
    rows = sol_ref.shape[0]
    half = nx_len // 2
    index = pl.program_id(0)
    steps = rows // some

    @pl.when(index == 0)
    def _():
        pltpu.make_async_copy(lower_in, lower_ref, sems.at[0]).start()
        pltpu.make_async_copy(upper_in, upper_ref, sems.at[1]).start()
        value_ref[...] = jnp.zeros_like(value_ref)
        state_ref[...] = jnp.ones_like(state_ref)

    field = rhs_ref[...].reshape(some * span, nx_len)
    first, second = field[:, :half], field[:, half:]
    parts = []
    for parity, folded in enumerate((first + second, first - second)):
        parts.append(dot3(halves(folded), (stream_ref[0, parity], stream_ref[1, parity]), ((1,), (0,))))
    lane = lax.broadcasted_iota(jnp.int32, (1, nx_len), 1)
    scale = jnp.where(lane == 0, 1.0 / nx_len, 2.0 / nx_len)
    modes = jnp.concatenate(parts, axis=1) * scale
    modes = dot3((sine_ref[0], sine_ref[1]), halves(modes), ((1,), (0,)))
    rows_ref[...] = modes.reshape(some, span, nx_len)

    @pl.when(index == 0)
    def _():
        pltpu.make_async_copy(lower_in, lower_ref, sems.at[0]).wait()
        pltpu.make_async_copy(upper_in, upper_ref, sems.at[1]).wait()

    base = place_ref[1] * rows
    sigma = sigma_ref[...]
    step = 8

    def descend(chunk, carry):
        value, numer, denom = carry
        for k in range(step):
            row = chunk * step + k
            cell = index * some + row
            low, high = lower_ref[base + cell], upper_ref[base + cell]
            numer = low * numer + sigma * denom
            new = numer + high * denom
            inv = denom / new
            denom = new
            inv_ref[row] = inv
            ratio_ref[cell] = high * inv
            value = (low * value - rows_ref[row]) * wide(inv)
            sol_ref[cell] = value
        return value, numer, denom

    value, numer, denom = lax.fori_loop(
        0, some // step, descend, (value_ref[...], state_ref[0], state_ref[1])
    )
    value_ref[...] = value
    state_ref[0] = numer
    state_ref[1] = denom

    @pl.when(index == steps - 1)
    def _():
        weight = weight_ref[0] * (2.0 / ((span + 1) * span_weight))

        def ascend(chunk, value):
            for k in range(step):
                row = rows - 1 - (chunk * step + k)
                value = sol_ref[row] + wide(ratio_ref[row]) * value
                sol_ref[row] = value
                part = weight * value
                part = part[: span // 2] + part[span // 2 :]
                part = part + pltpu.roll(part, 4, 0)
                part = part + pltpu.roll(part, 2, 0)
                other = pltpu.roll(part, 1, 0)
                edges_ref[pl.ds(row, 1)] = (part + other)[:1]
                edges_ref[pl.ds(rows + row, 1)] = (part - other)[:1]
            return value

        lax.fori_loop(0, rows // step, ascend, jnp.zeros((span, nx_len), jnp.float32))
        sines = (sine_ref[0, :span, :span], sine_ref[1, :span, :span])
        for side, row in enumerate((0, rows - 1)):
            edge = dot3(sines, halves(sol_ref[row]), ((1,), (0,))) * (2.0 / (span + 1))
            edges_ref[2 * rows + side * span : 2 * rows + side * span + span] = edge
        groups, both_parts, _ = send_ref.shape
        count = both_parts // 2
        quarter = nx_len // 4
        for tile in range(4):
            turned = edges_ref[:, tile * quarter : tile * quarter + quarter].T
            place = tile // 2 * (groups // 2)
            part = tile % 2 * count
            send_ref[place : place + groups // 2, part : part + count] = turned.reshape(groups // 2, count, -1)


def local_inverse(place_ref, lower_ref, upper_ref, piece_ref, rows_ref, inv_ref, weight_ref, stream_ref, sine_ref, out_ref, sol_ref, edges_ref, value_ref):
    rows, span, nx_len = rows_ref.shape
    some = out_ref.shape[0]
    half = nx_len // 2
    index = pl.program_id(0)
    steps = rows // some
    base = place_ref[1] * rows

    def ascend(chunk, value):
        for row in reversed(range(chunk * some, chunk * some + some)):
            value = sol_ref[row] + wide(upper_ref[base + row] * inv_ref[row]) * value
            sol_ref[row] = value
        value_ref[...] = value

    @pl.when(index == 0)
    def _():
        groups, both_parts, _ = piece_ref.shape
        count = both_parts // 2
        quarter = nx_len // 4
        for tile in range(4):
            place = tile // 2 * (groups // 2)
            part = tile % 2 * count
            block = piece_ref[place : place + groups // 2, part : part + count]
            edges_ref[:, tile * quarter : tile * quarter + quarter] = block.reshape(quarter, -1).T
        sines = (sine_ref[0, :span, :span], sine_ref[1, :span, :span])
        before = dot3(sines, halves(edges_ref[2 * rows : 2 * rows + span]), ((1,), (0,)))
        after = dot3(sines, halves(edges_ref[2 * rows + span :]), ((1,), (0,)))
        weight_low, weight_high = weight_ref[0], weight_ref[1]
        step = 8

        def descend(chunk, value):
            for k in range(step):
                row = chunk * step + k
                source = rows_ref[row] - weight_low * edges_ref[pl.ds(row, 1)] - weight_high * edges_ref[pl.ds(rows + row, 1)]
                value = (lower_ref[base + row] * value - source) * wide(inv_ref[row])
                sol_ref[row] = value
            return value

        lax.fori_loop(0, rows // step, descend, before)

        ascend(steps - 1, after)

    def transform(chunk):
        modes = sol_ref[chunk * some : chunk * some + some].reshape(some * span, nx_len)
        field = dot3((sine_ref[0], sine_ref[1]), halves(modes), ((1,), (0,))) * (2.0 / (span + 1))
        outs = []
        for parity in range(2):
            part = field[:, parity * half : parity * half + half]
            outs.append(dot3(halves(part), (stream_ref[0, parity], stream_ref[1, parity]), ((1,), (1,))))
        even, odd = outs
        out_ref[:, :, :half] = (even + odd).reshape(some, span, half)
        out_ref[:, :, half:] = (even - odd).reshape(some, span, half)

    for chunk in reversed(range(steps)):

        @pl.when(index == steps - 1 - chunk)
        def _(chunk=chunk):
            if chunk > 0:
                ascend(chunk - 1, value_ref[...])
            transform(chunk)


def factor(place_ref, lower_ref, upper_ref, waves_ref, both_ref, carry_down_ref, carry_up_ref, close_ref, start_ref):
    rows = both_ref.shape[1]
    blocks = carry_down_ref.shape[0]
    total = rows * blocks
    sigma = waves_ref[...]
    one = jnp.ones_like(sigma)
    step = 8

    def step_down(row, numer, denom):
        numer = lower_ref[row] * numer + sigma * denom
        return numer, numer + upper_ref[row] * denom

    def step_up(row, numer, denom):
        numer = upper_ref[row] * numer + sigma * denom
        return numer, numer + lower_ref[row] * denom

    def block(index, carry):
        t_down, t_up = carry
        other = blocks - 1 - index
        start_ref[0, index] = t_down
        start_ref[1, other] = t_up

        def some(chunk, inner):
            nd, dd, nu, du, prod_l, prod_u = inner
            for k in range(step):
                row = index * rows + chunk * step + k
                back = total - 1 - row
                nd, dd = step_down(row, nd, dd)
                nu, du = step_up(back, nu, du)
                prod_l = prod_l * lower_ref[row]
                prod_u = prod_u * upper_ref[back]
            return nd, dd, nu, du, prod_l, prod_u

        unit = jnp.float32(1.0)
        nd, dd, nu, du, prod_l, prod_u = lax.fori_loop(
            0, rows // step, some, (t_down, one, t_up, one, unit, unit)
        )
        inv_d = 1.0 / dd
        inv_u = 1.0 / du
        carry_down_ref[index] = prod_l * inv_d
        carry_up_ref[other] = prod_u * inv_u
        return nd * inv_d, nu * inv_u

    lax.fori_loop(0, blocks, block, (one, one))
    place = place_ref[1]
    first = place * rows

    def own(chunk, inner):
        nd, dd, nu, du = inner
        for k in range(step):
            row = chunk * step + k
            back = rows - 1 - row
            nd, new_d = step_down(first + row, nd, dd)
            both_ref[0, row] = dd / new_d
            nu, new_u = step_up(first + back, nu, du)
            both_ref[1, back] = du / new_u
            dd, du = new_d, new_u
        return nd, dd, nu, du

    nd, dd, nu, du = lax.fori_loop(
        0, rows // step, own, (start_ref[0, place], one, start_ref[1, place], one)
    )
    t_end = nd / dd
    t_next = start_ref[1, place]
    is_last = place == blocks - 1
    inner = jnp.where(is_last, 0.0, 1.0 / (t_next + t_end * (1.0 - t_next)))
    close_ref[0] = inner
    close_ref[1] = inner * (1.0 - t_next)
    close_ref[2] = 1.0 - start_ref[0, place]
    close_ref[3] = 1.0 - t_next


def span_forward(place_ref, lower_ref, upper_ref, piece_ref, factor_ref, close_ref, plane_ref, cell_ref, rows_ref, send_ref, edge_ref, keep_ref):
    groups, parts, lanes = piece_ref.shape
    rows, _, nz_len = rows_ref.shape
    span = nz_len // groups
    per = lanes // groups
    tiles = swap_bits([piece_ref[t] for t in range(groups)])
    lane = lax.broadcasted_iota(jnp.int32, (parts, lanes), 1)

    def source(value, group):
        return turn(tiles[value % groups], groups * (group - value // groups))

    for row in range(rows):
        pair = jnp.where(lane < groups, source(row, 0), source(rows + row, 1))
        keep_ref[row] = jnp.where(lane < 2 * groups, pair, 0.0)
    wave = lax.broadcasted_iota(jnp.int32, (1, nz_len), 1)
    scale = jnp.where(wave % (nz_len // 2) == 0, 1.0 / nz_len, 2.0 / nz_len)
    planes = keep_ref[...].reshape(rows * parts, lanes)
    spec = dot3(halves(planes), (plane_ref[0], plane_ref[1]), ((1,), (0,)))
    rows_ref[...] = (spec * (-span_weight * scale)).reshape(rows, parts, nz_len)
    cells = []
    for side in range(2):
        built = []
        for tile in range(nz_len // lanes):
            value = source(2 * rows + side * span + tile * per, 0)
            for group in range(1, per):
                other = source(2 * rows + side * span + tile * per + group, group)
                value = jnp.where(lane < groups * group, value, other)
            built.append(value)
        cells.append(jnp.concatenate(built, axis=1))
    edges = dot3(halves(jnp.concatenate(cells, axis=0)), (cell_ref[0], cell_ref[1]), ((1,), (0,))) * scale
    low_edge, high_edge = edges[:parts], edges[parts:]
    edge_ref[0] = low_edge
    edge_ref[1] = high_edge
    base = place_ref[1] * rows
    step = 8

    def sweep(chunk, carry):
        down, up = carry
        for k in range(step):
            row = chunk * step + k
            back = rows - 1 - row
            down = (lower_ref[base + row] * down - rows_ref[row]) * both(factor_ref[0, row])
            up = (upper_ref[base + back] * up - rows_ref[back]) * both(factor_ref[1, back])
        return down, up

    start = (both(close_ref[2]) * low_edge, both(close_ref[3]) * high_edge)
    down, up = lax.fori_loop(0, rows // step, sweep, start)
    send_ref[0] = down + high_edge
    send_ref[1] = up + low_edge


def span_inverse(place_ref, lower_ref, upper_ref, rows_ref, mate_ref, piece_ref, edge_ref, factor_ref, carry_down_ref, carry_up_ref, close_ref, plane_ref, cell_ref, *rest):
    *end_refs, out_ref, grow_ref, near_ref, ends_ref = rest
    groups, parts, lanes = out_ref.shape
    rows, _, nz_len = rows_ref.shape
    blocks = ends_ref.shape[0]
    span = nz_len // groups
    per = lanes // groups
    place = place_ref[1]
    base = place * rows
    step = 8
    zero = jnp.zeros((parts, nz_len), jnp.float32)
    pair = place // 2
    shifts = sorted(range(1, blocks), key=lambda d: min(d, blocks - d))
    for shift, end_ref in zip(shifts, end_refs):
        ends_ref[(pair + blocks - shift) % blocks] = end_ref[...]

    def rise(k, value):
        through = carry_down_ref[2 * k + 1] * carry_down_ref[2 * k]
        return ends_ref[k] + both(through) * value

    def climb(k, value):
        other = blocks - 1 - k
        through = carry_up_ref[2 * other + 1] * carry_up_ref[2 * other]
        return ends_ref[other] + both(through) * value

    before = lax.fori_loop(0, pair, rise, zero)
    after = lax.fori_loop(0, blocks - 1 - pair, climb, zero)
    odd = place % 2 == 1
    mate = jnp.where(odd, place - 1, place + 1)
    before = jnp.where(odd, mate_ref[0] + both(carry_down_ref[mate]) * before, before)
    after = jnp.where(odd, after, mate_ref[1] + both(carry_up_ref[mate]) * after)
    before = before + both(close_ref[2]) * edge_ref[0]
    after = after + both(close_ref[3]) * edge_ref[1]

    def descend(chunk, value):
        for k in range(step):
            row = chunk * step + k
            value = (lower_ref[base + row] * value - rows_ref[row]) * both(factor_ref[0, row])
            grow_ref[row] = value
        return value

    last = lax.fori_loop(0, rows // step, descend, before)
    beyond = both(close_ref[0]) * after + both(close_ref[1]) * last

    def ascend(chunk, value):
        for k in range(step):
            row = rows - 1 - (chunk * step + k)
            ratio = upper_ref[base + row] * factor_ref[0, row]
            value = grow_ref[row] + both(ratio) * value
            grow_ref[row] = value
        return value

    first = lax.fori_loop(0, rows // step, ascend, beyond)
    below = before + both(close_ref[2]) * first
    flat = grow_ref[...].reshape(rows * parts, nz_len)
    near = dot3(halves(flat), (plane_ref[0], plane_ref[1]), ((1,), (1,)))
    near_ref[...] = near.reshape(rows, parts, lanes)
    edges = jnp.concatenate([below, beyond], axis=0)
    cells = dot3(halves(edges), (cell_ref[0], cell_ref[1]), ((1,), (1,)))
    lane = lax.broadcasted_iota(jnp.int32, (parts, lanes), 1)
    def piece(value, group):
        if value < rows:
            return turn(near_ref[value], groups * group)
        if value < 2 * rows:
            return turn(near_ref[value - rows], groups * (group - 1))
        side, cell = divmod(value - 2 * rows, span)
        tile, part = divmod(cell, per)
        found = cells[side * parts : side * parts + parts, tile * lanes : tile * lanes + lanes]
        return turn(found, groups * (group - part))

    tiles = []
    for t in range(groups):
        value = piece(t, 0)
        for group in range(1, per):
            value = jnp.where(lane < groups * group, value, piece(groups * group + t, group))
        tiles.append(value)
    for t, value in enumerate(swap_bits(tiles)):
        left = turn(piece_ref[(t + groups - 1) % groups], -rows)
        right = turn(piece_ref[(t + 1) % groups], rows)
        own = jnp.where(lane < rows, left, jnp.where(lane < 2 * rows, right, 0.0))
        out_ref[t] = value + own


smem = pl.BlockSpec(memory_space=pltpu.SMEM)
vmem = pl.BlockSpec(memory_space=pltpu.VMEM)
far = pl.BlockSpec(memory_space=pl.ANY)


def local(rhs, lower, upper):
    rows, span, nx_len = rhs.shape
    groups = lax.axis_size("row")
    blocks = lax.axis_size("col")
    nz_len = span * groups
    modes = nx_len // 2 // groups
    parts = 2 * modes
    steps = 3
    some = rows // steps
    lanes = 2 * (rows + span)
    place = jnp.stack([lax.axis_index("row"), lax.axis_index("col")]).astype(jnp.int32)
    f32 = jnp.float32
    params = pltpu.CompilerParams(vmem_limit_bytes=40 * 1024 * 1024)
    stream = stream_table(nx_len)
    sines = split_table(np.kron(np.eye(some), sine_matrix(span)))
    plane = plane_table(nz_len, groups)
    plane = jnp.pad(plane, ((0, 0), (0, lanes - 2 * groups), (0, 0)))
    cell = cell_table(nz_len, groups)
    ends_of_block = sine_matrix(span)[[0, -1]] * span_weight
    weights = jnp.asarray(np.broadcast_to(ends_of_block[:, :, None], (2, span, nx_len)).astype(np.float32))

    def on_chip(*shape):
        return pltpu.VMEM(shape, f32)

    def on_hbm(value):
        return pltpu.with_memory_space_constraint(value, pltpu.HBM)

    def fixed(value):
        shape = value.shape
        return pl.BlockSpec(shape, lambda i: (0,) * len(shape))

    def exchange(value, axis):
        return lax.all_to_all(value, axis, split_axis=0, concat_axis=0, tiled=True)

    def stream_part(index):
        angle = 2.0 * math.pi / nx_len * index.astype(f32)
        return stream_weight * (2.0 - 2.0 * jnp.cos(angle))

    def span_part(index, count):
        angle = 2.0 * math.pi / count * index.astype(f32)
        return span_weight * (2.0 - 2.0 * jnp.cos(angle))

    quarter = nx_len // 4
    every = jnp.arange(nx_len // 2)
    kx = 2 * (every % quarter) + every // quarter
    kz = span_part(jnp.arange(1, span + 1), 2 * (span + 1))
    sigma_own = kz[:, None] + stream_part(kx)[None, :] + shift_value
    field_spec = pl.BlockSpec((some, span, nx_len), lambda i: (i, 0, 0))
    mode_spec = pl.BlockSpec((some, span, nx_len), lambda i: (i, 0, 0))
    inv_spec = pl.BlockSpec((some, span, nx_len // 2), lambda i: (i, 0, 0))
    own_rows, own_inv, send = pl.pallas_call(
        local_forward,
        grid=(steps,),
        in_specs=[smem, far, far, vmem, fixed(weights), field_spec, fixed(stream), fixed(sines)],
        out_specs=[mode_spec, inv_spec, vmem],
        out_shape=[
            pltpu.HBM((rows, span, nx_len), f32),
            pltpu.HBM((rows, span, nx_len // 2), f32),
            on_chip(groups, parts, lanes),
        ],
        scratch_shapes=[
            on_chip(rows, span, nx_len),
            on_chip(rows, span, nx_len // 2),
            on_chip(span, nx_len),
            on_chip(2, span, nx_len // 2),
            on_chip(lanes, nx_len),
            pltpu.SMEM(lower.shape, f32),
            pltpu.SMEM(upper.shape, f32),
            pltpu.SemaphoreType.DMA((2,)),
        ],
        compiler_params=params,
        name="local_forward",
    )(place, on_hbm(lower), on_hbm(upper), sigma_own, on_hbm(weights), on_hbm(rhs), on_hbm(stream), on_hbm(sines))
    piece = exchange(send, "row")

    order = place[0] * modes + jnp.arange(modes)
    kx = 2 * (order % quarter) + order // quarter
    kz = jnp.asarray(span_waves(nz_len).astype(np.int32))
    sigma = stream_part(kx)[:, None] + span_part(kz, nz_len)[None, :] + shift_value
    factors, carry_down, carry_up, close = pl.pallas_call(
        factor,
        in_specs=[smem, smem, smem, vmem],
        out_specs=[vmem] * 4,
        out_shape=[
            on_chip(2, rows, modes, nz_len),
            on_chip(blocks, modes, nz_len),
            on_chip(blocks, modes, nz_len),
            on_chip(4, modes, nz_len),
        ],
        scratch_shapes=[on_chip(2, blocks, modes, nz_len)],
        compiler_params=params,
        name="factor",
    )(place, lower, upper, sigma)

    mode_rows, ends, edges = pl.pallas_call(
        span_forward,
        in_specs=[smem, smem, smem] + [vmem] * 5,
        out_specs=[vmem] * 3,
        out_shape=[
            on_chip(rows, parts, nz_len),
            on_chip(2, parts, nz_len),
            on_chip(2, parts, nz_len),
        ],
        scratch_shapes=[on_chip(rows, parts, lanes)],
        compiler_params=params,
        name="span_forward",
    )(place, lower, upper, piece, factors, close, plane, cell)
    mate = lax.ppermute(ends, "col", [(k, k ^ 1) for k in range(blocks)])
    odd = place[1] % 2 == 1
    pair = place[1] // 2

    def twice(value):
        return jnp.concatenate([value, value], axis=0)

    lower_ends, upper_ends = jnp.where(odd, mate, ends), jnp.where(odd, ends, mate)
    through_down = lax.dynamic_index_in_dim(carry_down, 2 * pair + 1, 0, keepdims=False)
    through_up = lax.dynamic_index_in_dim(carry_up, 2 * pair, 0, keepdims=False)
    down = upper_ends[0] + twice(through_down) * lower_ends[0]
    up = lower_ends[1] + twice(through_up) * upper_ends[1]
    chips = blocks // 2
    ends = []
    for shift in sorted(range(1, chips), key=lambda d: min(d, chips - d)):
        message = jnp.where(pair + shift < chips, down, up)
        route = [(k, (k + 2 * shift) % blocks) for k in range(blocks)]
        ends.append(lax.ppermute(message, "col", route))

    send = pl.pallas_call(
        span_inverse,
        in_specs=[smem, smem, smem] + [vmem] * (10 + len(ends)),
        out_specs=vmem,
        out_shape=on_chip(groups, parts, lanes),
        scratch_shapes=[
            on_chip(rows, parts, nz_len),
            on_chip(rows, parts, lanes),
            on_chip(chips, parts, nz_len),
        ],
        compiler_params=params,
        name="span_inverse",
    )(place, lower, upper, mode_rows, mate, piece, edges, factors, carry_down, carry_up, close, plane, cell, *ends)
    piece = exchange(send, "row")

    return pl.pallas_call(
        local_inverse,
        grid=(steps,),
        in_specs=[smem, smem, smem] + [vmem] * 6,
        out_specs=pl.BlockSpec((some, span, nx_len), lambda i: (steps - 1 - i, 0, 0)),
        out_shape=jax.ShapeDtypeStruct((rows, span, nx_len), f32),
        scratch_shapes=[on_chip(rows, span, nx_len), on_chip(lanes, nx_len), on_chip(span, nx_len)],
        compiler_params=params,
        name="local_inverse",
    )(place, lower, upper, piece, own_rows, own_inv, weights, stream, sines)


def solution(mesh):
    return jax.shard_map(
        local,
        mesh=mesh,
        in_specs=(P("col", "row", None), P(), P()),
        out_specs=P("col", "row", None),
        check_vma=False,
    )
```
